128 devices in a mesh: seq: 8 (over y, core), exp: 16 (over z, x).
Axes of the slice: x: 4, y: 4, z: 4, core: 2. Of those that a mesh axis runs over, the one named last changes fastest.
Arguments:
- resid: bfloat16 [16, 1024, 4096], P('exp', 'seq'), may hold values from -1.5 to 1.5
- queries: bfloat16 [16, 1024, 4096], P('exp', 'seq'), may hold values from -8 to 8
- span_rotated_keys: bfloat16 [16, 1024, 512], P('exp', 'seq'), may hold values from -6 to 6
- span_value_rows: bfloat16 [16, 1024, 512], P('exp', 'seq'), may hold values from -6 to 6
- key_cache: bfloat16 [16, 4, 512, 128], P('exp', None, 'seq'), may hold values from -8 to 8
- prefix_value_cache: bfloat16 [16, 4, 512, 128], P('exp', None, 'seq'), may hold values from -6 to 6
- prefix_len: int32 [16], P('exp'), may hold values from 1 to 512, as said below
- out_weight: bfloat16 [4096, 4096], P('seq'), may hold values from -0.09375 to 0.09375
- norm_gain: float32 [4096], replicated, may hold values from 0.1 to 1.9
- router_weight: bfloat16 [4096, 128], replicated
- expert_ids: int32 [16, 1024, 8], P('exp', 'seq'), may hold values from 0 to 127, all different within a row; in each aligned block of 128 rows (0 to 127, 128 to 255, ..., all dimensions but the last counted through in order) at most 9 rows name the same one
- w_gate: bfloat16 [128, 4096, 768], P(('seq', 'exp')), may hold values from -0.09375 to 0.09375
- w_up: bfloat16 [128, 4096, 768], P(('seq', 'exp')), may hold values from -0.09375 to 0.09375
- w_down: bfloat16 [128, 768, 4096], P(('seq', 'exp')), may hold values from -0.21875 to 0.21875
Outputs:
- layer_out: bfloat16 [16, 1024, 4096], P('exp', 'seq')
The draws below stay inside these ranges and needn't reach their ends.
Inputs may be any that keep to these rules, and one draw needn't show every extreme that they name: `expert_ids`: in the 128 consecutive tokens of one index of seq, no expert is named by more than 9 routes, a bound that some block reaches. `prefix_len`: some prompt's prefix fills the cache.
All inputs are finite; a program needn't handle non-finite values.
Results may differ from the reference program's by a relative error of at most 0.03.
Values may be sent and summed in bfloat16 or wider, within the bound.
No kernel may reach another device: no remote copies, remote signals or barrier semaphores. Data moves between devices by JAX's collectives and lax.ppermute only.
A program may use at most 192 MiB of HBM per device.

```python
import math
import jax
import jax.numpy as jnp
import numpy as np
from jax import lax

D = 4096
QUERY_HEAD_HALF = 32
KEY_VALUE_HEADS = 4
HEAD_SIZE = 128
FF = 768
TOP = 8
TOK_DEV = 128
PROMPT_COUNT = 16
SPAN_TOKENS = 1024
PREFIX_CAPACITY = 512
EXPERTS = 128
CAP = 9
N_SEQ = 8


def draw_queries(key, part):
    offset_start = jnp.clip(jax.random.normal(jax.random.fold_in(key, 21), (PROMPT_COUNT, SPAN_TOKENS, QUERY_HEAD_HALF, HEAD_SIZE), jnp.float32), -6.0, 6.0)
    return offset_start.reshape(PROMPT_COUNT, SPAN_TOKENS, QUERY_HEAD_HALF * HEAD_SIZE).astype(jnp.bfloat16)


def draw_key_cache(key, part):
    offset_start = jnp.clip(jax.random.normal(jax.random.fold_in(key, 31), (PROMPT_COUNT, KEY_VALUE_HEADS, PREFIX_CAPACITY, HEAD_SIZE), jnp.float32), -6.0, 6.0)
    return offset_start.astype(jnp.bfloat16)


def draw_router_weight(key, part):
    offset_start = jnp.clip(jax.random.normal(jax.random.fold_in(key, 41), (D, EXPERTS), jnp.float32), -4.0, 4.0) * D ** (-0.5)
    return offset_start.astype(jnp.bfloat16)


def draw_prefix_len(key, part):
    lengths = jax.random.randint(jax.random.fold_in(key, 51), (PROMPT_COUNT,), 1, PREFIX_CAPACITY + 1)
    chosen = jax.random.randint(jax.random.fold_in(key, 52), (), 0, PROMPT_COUNT)
    return jnp.where(jnp.arange(PROMPT_COUNT) == chosen, PREFIX_CAPACITY, lengths).astype(jnp.int32)


def level_of(key, extent, split, least, high):
    def one(dim, shards_of):
        draws = jax.random.uniform(jax.random.fold_in(jax.random.fold_in(key, 6), dim), (shards_of,), jnp.float32, least / len(split), high / len(split))
        return jnp.repeat(jnp.exp(draws), extent[dim] // shards_of).reshape((-1,) + (1,) * (len(extent) - dim - 1))

    level = one(*split[0])
    for cut in split[1:]:
        level = level * one(*cut)
    return level


def deal_out(key, own, number, rows, number_of, top, bound, lean):
    ranking = jax.random.permutation(key, number_of)
    heavy_load, usual = shares(number_of, rows * top, bound, lean, True), shares(number_of, rows * top, bound, lean, False)
    places = jnp.arange(number_of)

    def named(sizes, offset_by):
        used = int((sizes > 0).sum())
        fixed = max(1, used // 4)
        passed = fixed + (places - fixed + offset_by * (used - fixed)) % max(1, number_of - fixed)
        return jnp.zeros((number_of,), jnp.int32).at[ranking[jnp.where(places < fixed, places, passed)]].set(jnp.asarray(sizes, jnp.int32))

    sizes = jnp.where(number % 4 == 0, named(heavy_load, number // 4), named(usual, number - number // 4 - 1))
    mixed = jax.random.permutation(jax.random.fold_in(own, 3), number_of)
    source_of, taker = mixed[0:number_of // 2 * 2:2], mixed[1:number_of // 2 * 2:2]
    slack = jnp.minimum(sizes[source_of] - 1, bound - sizes[taker]) // 2
    slack = jnp.where((source_of == ranking[0]) | (taker == ranking[0]) | (sizes[taker] == 0), 0, jnp.maximum(slack, 0))
    passed = jax.random.randint(jax.random.fold_in(own, 4), (number_of // 2,), 0, 1 << 20) % (slack + 1)
    sizes = sizes.at[source_of].add(-passed).at[taker].add(passed)
    items = jnp.searchsorted(jnp.cumsum(sizes), jnp.arange(rows * top), side="right").astype(jnp.int32)
    grid = items.reshape(top, rows).T
    grid = grid[jax.random.permutation(jax.random.fold_in(own, 1), rows)]
    offset_by = jax.random.randint(jax.random.fold_in(own, 2), (rows, 1), 0, top)
    return jnp.take_along_axis(grid, (jnp.arange(top)[None, :] + offset_by) % top, axis=1)


def shares(number_of, total, reach, slope, full):
    loads = [(1 << 20) // math.isqrt(grade ** slope) + 1 for grade in range(1, number_of + 1)]
    largest = reach if full else min(reach, max(-(-total // number_of), total * loads[0] // sum(loads)))
    least = 1 if total - largest >= number_of - 1 else 0
    counts, surplus = [largest] + [least] * (number_of - 1), total - largest - least * (number_of - 1)
    while surplus > 0:
        movable = [i for i in range(1, number_of) if counts[i] < largest] or [i for i in range(1, number_of) if counts[i] < reach]
        whole, remaining = sum([loads[i] for i in movable]), surplus
        for i in movable:
            more = min(reach - counts[i], max(1, remaining * loads[i] // whole), surplus)
            counts[i] = counts[i] + more
            surplus = surplus - more
    return np.array(counts)


def normal_values(own_key, dims, scale, limit, shards=(), held_as=jnp.bfloat16):
    loudness = level_of(own_key, dims, shards, -0.22, 0.18) if shards else 1.0
    entries = jax.random.normal(own_key, dims, jnp.float32) * scale * loudness
    return jnp.minimum(jnp.maximum(entries, -limit), limit).astype(held_as)


def setup_inputs(seed: int = 0) -> dict:
    streams_of = jax.random.split(jax.random.key(seed), 15)
    resid = normal_values(streams_of[0], (PROMPT_COUNT, SPAN_TOKENS, D), 0.25, 1.5, ((0, 16), (1, 8)))
    queries = draw_queries(jax.random.fold_in(streams_of[14], 71), 0)
    span_rotated_keys = normal_values(streams_of[2], (PROMPT_COUNT, SPAN_TOKENS, KEY_VALUE_HEADS * HEAD_SIZE), 1.0, 6.0, ((0, 16), (1, 8)))
    span_value_rows = normal_values(streams_of[3], (PROMPT_COUNT, SPAN_TOKENS, KEY_VALUE_HEADS * HEAD_SIZE), 1.0, 6.0, ((0, 16), (1, 8)))
    key_cache = draw_key_cache(jax.random.fold_in(streams_of[14], 71), 0)
    prefix_value_cache = normal_values(streams_of[5], (PROMPT_COUNT, KEY_VALUE_HEADS, PREFIX_CAPACITY, HEAD_SIZE), 1.0, 6.0, ((0, 16), (2, 8)))
    prefix_len = draw_prefix_len(jax.random.fold_in(streams_of[14], 71), 0)
    out_weight = normal_values(streams_of[7], (QUERY_HEAD_HALF * HEAD_SIZE, D), (QUERY_HEAD_HALF * HEAD_SIZE) ** -0.5, 0.09375, ((0, 8),))
    norm_gain = jnp.clip(1.0 + 0.18 * jax.random.normal(streams_of[8], (D,), jnp.float32), 0.1, 1.9)
    router_weight = draw_router_weight(jax.random.fold_in(streams_of[14], 71), 0)
    expert_ids_keys = jax.random.split(jax.random.fold_in(streams_of[10], 1), PROMPT_COUNT * SPAN_TOKENS // TOK_DEV)
    expert_ids_turns = jax.random.permutation(jax.random.fold_in(streams_of[10], 3), PROMPT_COUNT * SPAN_TOKENS // TOK_DEV)
    expert_ids = jax.vmap(lambda own, number: deal_out(jax.random.fold_in(streams_of[10], 2), own, number, TOK_DEV, EXPERTS, TOP, CAP, 2))(expert_ids_keys, expert_ids_turns).reshape((PROMPT_COUNT, SPAN_TOKENS, TOP))
    w_gate = normal_values(streams_of[11], (EXPERTS, D, FF), D ** -0.5, 0.09375, ((0, 128),))
    w_up = normal_values(streams_of[12], (EXPERTS, D, FF), D ** -0.5, 0.09375, ((0, 128),))
    w_down = normal_values(streams_of[13], (EXPERTS, FF, D), FF ** -0.5, 0.21875, ((0, 128),))
    return dict(resid=resid, queries=queries, span_rotated_keys=span_rotated_keys, span_value_rows=span_value_rows, key_cache=key_cache, prefix_value_cache=prefix_value_cache, prefix_len=prefix_len, out_weight=out_weight, norm_gain=norm_gain, router_weight=router_weight, expert_ids=expert_ids, w_gate=w_gate, w_up=w_up, w_down=w_down)


def expert_mlp(token_rows, gate_part, up_part, down_part):
    gate_val = jnp.dot(token_rows, gate_part, preferred_element_type=jnp.float32)
    up_val = jnp.dot(token_rows, up_part, preferred_element_type=jnp.float32)
    activated = (jax.nn.silu(gate_val) * up_val).astype(jnp.bfloat16)
    return jnp.dot(activated, down_part, preferred_element_type=jnp.float32).astype(jnp.bfloat16)

def attend_prompt(inputs):
    query_one, single_prompt_keys, single_prompt_values, cache_keys, cache_values, length = inputs
    group_length = QUERY_HEAD_HALF // KEY_VALUE_HEADS
    span_length = query_one.shape[0]
    prefix_total = cache_keys.shape[1]
    query_block = query_one.reshape(span_length, QUERY_HEAD_HALF, HEAD_SIZE).astype(jnp.float32)
    spanned_key_rows = single_prompt_keys.reshape(span_length, KEY_VALUE_HEADS, HEAD_SIZE).transpose(1, 0, 2)
    spanned_value_rows = single_prompt_values.reshape(span_length, KEY_VALUE_HEADS, HEAD_SIZE).transpose(1, 0, 2)
    all_keys = jnp.repeat(jnp.concatenate([cache_keys, spanned_key_rows], axis=1), group_length, axis=0).astype(jnp.float32)
    all_values = jnp.repeat(jnp.concatenate([cache_values, spanned_value_rows], axis=1), group_length, axis=0).astype(jnp.float32)
    scores = jnp.einsum('thd,hjd->htj', query_block, all_keys) * HEAD_SIZE ** (-0.5)
    position = jnp.arange(prefix_total + span_length, dtype=jnp.int32)
    query_pos = jnp.arange(span_length, dtype=jnp.int32)
    usable_keys = jnp.where(position[None, :] < prefix_total, position[None, :] < length, position[None, :] - prefix_total <= query_pos[:, None])
    scores = jnp.where(usable_keys[None], scores, -1e+30)
    top_score = lax.optimization_barrier(jnp.max(scores, axis=2, keepdims=True))
    raised = jnp.exp(scores - top_score)
    attn_weights = (raised / lax.optimization_barrier(jnp.sum(raised, axis=2, keepdims=True))).astype(jnp.bfloat16)
    attended = jnp.einsum('htj,hjd->thd', attn_weights.astype(jnp.float32), all_values).astype(jnp.bfloat16)
    return attended.reshape(span_length, QUERY_HEAD_HALF * HEAD_SIZE)

def reference(resid, queries, span_rotated_keys, span_value_rows, key_cache, prefix_value_cache, prefix_len, out_weight, norm_gain, router_weight, expert_ids, w_gate, w_up, w_down):
    attended = lax.map(attend_prompt, (queries, span_rotated_keys, span_value_rows, key_cache, prefix_value_cache, prefix_len))
    token_total = PROMPT_COUNT * SPAN_TOKENS
    flat_attn = attended.reshape(token_total, QUERY_HEAD_HALF * HEAD_SIZE)
    group_width = QUERY_HEAD_HALF * HEAD_SIZE // N_SEQ
    projected = jnp.zeros((token_total, D), jnp.float32)
    for group_index in range(N_SEQ):
        lower = group_index * group_width
        partial_sum = jnp.dot(flat_attn[:, lower:lower + group_width], out_weight[lower:lower + group_width], preferred_element_type=jnp.float32).astype(jnp.bfloat16)
        projected = projected + lax.optimization_barrier(partial_sum).astype(jnp.float32)
    hidden_state = resid.reshape(token_total, D).astype(jnp.float32) + projected
    mean_square = lax.optimization_barrier(jnp.mean(hidden_state * hidden_state, axis=1, keepdims=True))
    normed = (hidden_state * lax.rsqrt(mean_square + 1e-06) * norm_gain).astype(jnp.bfloat16)
    logits = jnp.dot(normed, router_weight, preferred_element_type=jnp.float32)
    chosen_ids = expert_ids.reshape(token_total, TOP)
    chosen = jnp.take_along_axis(logits, chosen_ids, axis=1)
    route_weight = jax.nn.softmax(chosen, axis=1)
    block_count = token_total // TOK_DEV
    per_block = TOK_DEV * TOP
    flat_ids = chosen_ids.reshape(block_count, per_block)
    one_hot = (flat_ids[:, :, None] == jnp.arange(EXPERTS, dtype=jnp.int32)[None, None, :]).astype(jnp.int32)
    running_rank = jnp.cumsum(one_hot, axis=1) - 1
    slot_index = lax.optimization_barrier(jnp.sum(one_hot * running_rank, axis=2))
    block_ids = jnp.arange(block_count, dtype=jnp.int32)[:, None]
    buffer_len = block_count * CAP
    target = flat_ids * buffer_len + block_ids * CAP + slot_index
    source_token = block_ids * TOK_DEV + jnp.arange(per_block, dtype=jnp.int32)[None, :] // TOP
    slot_token = jnp.full((EXPERTS * buffer_len,), token_total, jnp.int32).at[target.reshape(-1)].set(source_token.reshape(-1))
    slot_weight = jnp.zeros((EXPERTS * buffer_len,), jnp.float32).at[target.reshape(-1)].set(route_weight.reshape(-1))
    padded = jnp.concatenate([normed, jnp.zeros((1, D), jnp.bfloat16)], axis=0)

    def add_expert(mixture, inputs):
        token_list, weight_list, gate_part, up_part, down_part = inputs
        outputs = expert_mlp(padded[token_list], gate_part, up_part, down_part).astype(jnp.float32)
        return (mixture.at[token_list].add(weight_list[:, None] * outputs, mode='drop'), None)
    mixture, unused = lax.scan(add_expert, jnp.zeros((token_total, D), jnp.float32), (slot_token.reshape(EXPERTS, buffer_len), slot_weight.reshape(EXPERTS, buffer_len), w_gate, w_up, w_down))
    return (hidden_state + mixture).astype(jnp.bfloat16).reshape(PROMPT_COUNT, SPAN_TOKENS, D)
```

```python
import functools

import jax
import jax.numpy as jnp
import numpy as np
from jax import lax
from jax.experimental import pallas as pl
from jax.experimental.pallas import tpu as pltpu
from jax.sharding import PartitionSpec as P

QUERY_HEAD_HALF = 32
KEY_VALUE_HEADS = 4
HEAD_SIZE = 128
TOP = 8
SLOTS = 8
MIB = 1 << 20


def dot(a, b):
    return jnp.dot(a, b, preferred_element_type=jnp.float32)


def dot_nt(a, b):
    return lax.dot_general(a, b, (((1,), (1,)), ((), ())), preferred_element_type=jnp.float32)


def spread(experts):
    rows = lax.broadcasted_iota(jnp.int32, (experts * SLOTS, experts), 0)
    cols = lax.broadcasted_iota(jnp.int32, (experts * SLOTS, experts), 1)
    return jnp.where(rows // SLOTS == cols, 1.0, 0.0).astype(jnp.bfloat16)


def route_kernel(
    resid_ref, proj_ref, gain_ref, router_ref, ids_ref,
    send_ref, rank_ref, weight_ref,
    normed_ref, pick_ref,
):
    step = pl.program_id(0)
    tokens, width = resid_ref.shape
    experts = router_ref.shape[1]
    cols = send_ref.shape[1]
    extra = width // cols

    @pl.when(step == 0)
    def _():
        hidden = resid_ref[...].astype(jnp.float32) + proj_ref[...].astype(jnp.float32)
        mean_square = jnp.mean(hidden * hidden, axis=1, keepdims=True)
        normed = (hidden * lax.rsqrt(mean_square + 1e-06) * gain_ref[...]).astype(jnp.bfloat16)
        for j in range(extra):
            normed_ref[pl.ds(j * tokens, tokens), :] = normed[:, j * cols : (j + 1) * cols]
        logits = dot(normed, router_ref[...])
        lane = lax.broadcasted_iota(jnp.int32, (tokens, experts), 1)
        named = jnp.zeros((tokens, experts), jnp.bool_)
        for k in range(TOP):
            named = named | (ids_ref[:, k : k + 1] == lane)
        masked = jnp.where(named, logits, -jnp.inf)
        top = jnp.max(masked, axis=1, keepdims=True)
        raised = jnp.where(named, jnp.exp(logits - top), 0.0)
        weight_ref[...] = raised / jnp.sum(raised, axis=1, keepdims=True)
        earlier = jnp.where(
            lax.broadcasted_iota(jnp.int32, (tokens, tokens), 0)
            > lax.broadcasted_iota(jnp.int32, (tokens, tokens), 1),
            1.0,
            0.0,
        ).astype(jnp.bfloat16)
        member = jnp.where(named, 1.0, 0.0).astype(jnp.bfloat16)
        rank = jnp.where(named, dot(earlier, member) + 1.0, 0.0)
        rank_ref[...] = rank
        wide_rank = dot_nt(spread(experts), rank.astype(jnp.bfloat16))
        slot = (
            lax.broadcasted_iota(jnp.int32, (experts * SLOTS, tokens), 0) % SLOTS
        ).astype(jnp.float32)
        pick_ref[:, pl.ds(0, tokens)] = jnp.where(wide_rank == slot + 1.0, 1.0, 0.0).astype(
            jnp.bfloat16
        )
        for j in range(extra):
            pick_ref[:, pl.ds((j + 1) * tokens, tokens)] = jnp.where(
                (wide_rank == SLOTS + 1.0) & (slot == j), 1.0, 0.0
            ).astype(jnp.bfloat16)

    @pl.when(step < extra)
    def _():
        start = pl.multiple_of(jnp.minimum(step, extra - 1) * tokens, tokens)
        send_ref[...] = dot(
            pick_ref[:, pl.ds(0, tokens)], normed_ref[pl.ds(start, tokens), :]
        ).astype(jnp.bfloat16)

    @pl.when(step == extra)
    def _():
        send_ref[...] = dot(
            pick_ref[:, pl.ds(tokens, extra * tokens)], normed_ref[...]
        ).astype(jnp.bfloat16)


def route(resid, projected, gain, router, ids):
    tokens, width = resid.shape
    experts = router.shape[1]
    cols = width // SLOTS
    whole = lambda shape: pl.BlockSpec(shape, lambda j: (0, 0))
    return pl.pallas_call(
        route_kernel,
        grid=(SLOTS + 1,),
        in_specs=[
            whole((tokens, width)),
            whole((tokens, width)),
            whole((1, width)),
            whole((width, experts)),
            whole((tokens, TOP)),
        ],
        out_specs=[
            pl.BlockSpec((experts * SLOTS, cols), lambda j: (0, j)),
            whole((tokens, experts)),
            whole((tokens, experts)),
        ],
        out_shape=[
            jax.ShapeDtypeStruct((experts * SLOTS, width + cols), jnp.bfloat16),
            jax.ShapeDtypeStruct((tokens, experts), jnp.float32),
            jax.ShapeDtypeStruct((tokens, experts), jnp.float32),
        ],
        scratch_shapes=[
            pltpu.VMEM((SLOTS * tokens, cols), jnp.bfloat16),
            pltpu.VMEM((experts * SLOTS, (SLOTS + 1) * tokens), jnp.bfloat16),
        ],
        compiler_params=pltpu.CompilerParams(vmem_limit_bytes=48 * MIB),
        name="route",
    )(resid, projected, gain, router, ids)


def expert_kernel(
    rows_ref, extra_ref, gate_ref, up_ref, down_ref, out_ref, gate_acc, up_acc, act_ref, last_ref
):
    step = pl.program_id(0)
    blocks = SLOTS
    main, cols = rows_ref.shape
    sources = main // SLOTS

    def lane_pick(j):
        source = lax.broadcasted_iota(jnp.int32, (sources, main), 0)
        column = lax.broadcasted_iota(jnp.int32, (sources, main), 1)
        return jnp.where(column == source * SLOTS + j, 1.0, 0.0).astype(jnp.bfloat16)

    @pl.when(step < blocks)
    def _():
        ninth = dot(lane_pick(step), extra_ref[...]).astype(jnp.bfloat16)
        rows = jnp.concatenate([rows_ref[...], ninth], axis=0)
        gate_part, up_part = dot(rows, gate_ref[0]), dot(rows, up_ref[0])

        @pl.when(step == 0)
        def _():
            gate_acc[...] = gate_part
            up_acc[...] = up_part

        @pl.when(step > 0)
        def _():
            gate_acc[...] += gate_part
            up_acc[...] += up_part

    @pl.when(step == blocks - 1)
    def _():
        gate_val = gate_acc[...]
        act_ref[...] = (gate_val / (1.0 + jnp.exp(-gate_val)) * up_acc[...]).astype(jnp.bfloat16)
        last_ref[...] = jnp.zeros_like(last_ref)

    @pl.when((step >= blocks) & (step < 2 * blocks))
    def _():
        result = dot(act_ref[...], down_ref[0]).astype(jnp.bfloat16)
        out_ref[...] = result[:main]
        j = step - blocks
        row = lax.broadcasted_iota(jnp.int32, (main, sources), 0)
        source = lax.broadcasted_iota(jnp.int32, (main, sources), 1)
        place = jnp.where(row == source * SLOTS + j, 1.0, 0.0).astype(jnp.bfloat16)
        last_ref[...] += dot(place, result[main:])

    @pl.when(step == 2 * blocks)
    def _():
        out_ref[...] = last_ref[...].astype(jnp.bfloat16)


def expert(rows, w_gate, w_up, w_down):
    main = rows.shape[0]
    _, width, hidden = w_gate.shape
    cols = width // SLOTS
    tall = main + main // SLOTS
    first = lambda s: jnp.minimum(s, SLOTS - 1)
    second = lambda s: jnp.clip(s - SLOTS, 0, SLOTS - 1)
    return pl.pallas_call(
        expert_kernel,
        grid=(2 * SLOTS + 1,),
        in_specs=[
            pl.BlockSpec((main, cols), lambda s: (0, first(s))),
            pl.BlockSpec((main, cols), lambda s: (0, SLOTS)),
            pl.BlockSpec((1, cols, hidden), lambda s: (0, first(s), 0)),
            pl.BlockSpec((1, cols, hidden), lambda s: (0, first(s), 0)),
            pl.BlockSpec((1, hidden, cols), lambda s: (0, 0, second(s))),
        ],
        out_specs=pl.BlockSpec((main, cols), lambda s: (0, jnp.clip(s - SLOTS, 0, SLOTS))),
        out_shape=jax.ShapeDtypeStruct(rows.shape, jnp.bfloat16),
        scratch_shapes=[
            pltpu.VMEM((tall, hidden), jnp.float32),
            pltpu.VMEM((tall, hidden), jnp.float32),
            pltpu.VMEM((tall, hidden), jnp.bfloat16),
            pltpu.VMEM((main, cols), jnp.float32),
        ],
        compiler_params=pltpu.CompilerParams(vmem_limit_bytes=52 * MIB),
        name="expert",
    )(rows, rows, w_gate, w_up, w_down)


def combine_kernel(
    rows_ref, extra_ref, rank_ref, weight_ref, resid_ref, proj_ref, out_ref, main_ref, ninth_ref
):
    step = pl.program_id(0)
    tokens, experts = rank_ref.shape

    @pl.when(step == 0)
    def _():
        rank = rank_ref[...]
        weight = weight_ref[...]
        high = weight.astype(jnp.bfloat16)
        low = (weight - high.astype(jnp.float32)).astype(jnp.bfloat16)
        picks = spread(experts)
        wide_rank = dot_nt(rank.astype(jnp.bfloat16), picks)
        slot = (
            lax.broadcasted_iota(jnp.int32, wide_rank.shape, 1) % SLOTS
        ).astype(jnp.float32)
        for half, part in enumerate((high, low)):
            wide = dot_nt(part, picks)
            rows = pl.ds(half * tokens, tokens)
            main_ref[rows, :] = jnp.where(wide_rank == slot + 1.0, wide, 0.0).astype(jnp.bfloat16)
            ninth_ref[rows, :] = jnp.where(wide_rank == SLOTS + 1.0, wide, 0.0).astype(
                jnp.bfloat16
            )

    slot = lax.broadcasted_iota(jnp.int32, ninth_ref.shape, 1) % SLOTS
    ninth = ninth_ref[...]
    ninth = jnp.where(slot == step, ninth, jnp.zeros_like(ninth))
    both = dot(main_ref[...], rows_ref[...]) + dot(ninth, extra_ref[...])
    hidden = resid_ref[...].astype(jnp.float32) + proj_ref[...].astype(jnp.float32)
    out_ref[...] = (hidden + (both[:tokens] + both[tokens:])).astype(jnp.bfloat16)


def combine(rows, rank, weight, resid, projected):
    tokens, width = resid.shape
    main = rows.shape[0]
    experts = rank.shape[1]
    cols = width // SLOTS
    return pl.pallas_call(
        combine_kernel,
        grid=(SLOTS,),
        in_specs=[
            pl.BlockSpec((main, cols), lambda j: (0, j)),
            pl.BlockSpec((main, cols), lambda j: (0, SLOTS)),
            pl.BlockSpec((tokens, experts), lambda j: (0, 0)),
            pl.BlockSpec((tokens, experts), lambda j: (0, 0)),
            pl.BlockSpec((tokens, cols), lambda j: (0, j)),
            pl.BlockSpec((tokens, cols), lambda j: (0, j)),
        ],
        out_specs=pl.BlockSpec((tokens, cols), lambda j: (0, j)),
        out_shape=jax.ShapeDtypeStruct((tokens, width), jnp.bfloat16),
        scratch_shapes=[
            pltpu.VMEM((2 * tokens, main), jnp.bfloat16),
            pltpu.VMEM((2 * tokens, main), jnp.bfloat16),
        ],
        compiler_params=pltpu.CompilerParams(vmem_limit_bytes=48 * MIB),
        name="combine",
    )(rows, rows, rank, weight, resid, projected)


def per_device(
    resid,
    queries,
    span_rotated_keys,
    span_value_rows,
    key_cache,
    prefix_value_cache,
    prefix_len,
    out_weight,
    norm_gain,
    router_weight,
    expert_ids,
    w_gate,
    w_up,
    w_down,
):
    seq_count = lax.axis_size("seq")
    token_row_block = queries.shape[1]
    model_width = resid.shape[2]
    heads_here = QUERY_HEAD_HALF // seq_count
    group_length = QUERY_HEAD_HALF // KEY_VALUE_HEADS
    key_value_choice = np.arange(seq_count) * heads_here // group_length
    query_parts = queries[0].reshape(token_row_block, seq_count, heads_here * HEAD_SIZE)
    newest_keys = span_rotated_keys[0].reshape(token_row_block, KEY_VALUE_HEADS, HEAD_SIZE)[
        :, key_value_choice, :
    ]
    newest_values = span_value_rows[0].reshape(token_row_block, KEY_VALUE_HEADS, HEAD_SIZE)[
        :, key_value_choice, :
    ]
    fresh_pairs = jnp.concatenate([newest_keys, newest_values], axis=2)
    query_heads, span_pairs = (
        lax.all_to_all(query_parts, "seq", split_axis=1, concat_axis=0, tiled=True),
        lax.all_to_all(fresh_pairs, "seq", split_axis=1, concat_axis=0, tiled=True),
    )
    cache_pairs = jnp.concatenate(
        [key_cache[0][key_value_choice], prefix_value_cache[0][key_value_choice]], axis=2
    )
    prefix_pairs = lax.all_to_all(cache_pairs, "seq", split_axis=0, concat_axis=1, tiled=True)[0]
    span_length = query_heads.shape[0]
    prefix_total = prefix_pairs.shape[0]
    all_keys = jnp.concatenate([prefix_pairs[:, :HEAD_SIZE], span_pairs[:, 0, :HEAD_SIZE]], axis=0)
    all_values = jnp.concatenate(
        [prefix_pairs[:, HEAD_SIZE:], span_pairs[:, 0, HEAD_SIZE:]], axis=0
    )
    query_block = query_heads.reshape(span_length, heads_here, HEAD_SIZE)
    scores = jnp.einsum(
        "thd,jd->htj", query_block, all_keys, preferred_element_type=jnp.float32
    ) * HEAD_SIZE ** (-0.5)
    position = jnp.arange(prefix_total + span_length, dtype=jnp.int32)
    query_pos = jnp.arange(span_length, dtype=jnp.int32)
    usable_keys = jnp.where(
        position[None, :] < prefix_total,
        position[None, :] < prefix_len[0],
        position[None, :] - prefix_total <= query_pos[:, None],
    )
    scores = jnp.where(usable_keys[None], scores, -1e30)
    top_score = jnp.max(scores, axis=2, keepdims=True)
    raised = jnp.exp(scores - top_score)
    attn_weights = (raised / jnp.sum(raised, axis=2, keepdims=True)).astype(jnp.bfloat16)
    attended = jnp.einsum(
        "htj,jd->thd", attn_weights, all_values, preferred_element_type=jnp.float32
    ).astype(jnp.bfloat16)
    attended = attended.reshape(span_length, heads_here * HEAD_SIZE)
    projected = lax.psum_scatter(
        jnp.dot(attended, out_weight, preferred_element_type=jnp.float32).astype(jnp.bfloat16),
        "seq",
        scatter_dimension=0,
        tiled=True,
    )
    experts = router_weight.shape[1]
    send, rank, weight = route(
        resid[0], projected, norm_gain.reshape(1, model_width), router_weight, expert_ids[0]
    )

    def exchange(rows):
        blocks = rows.reshape(experts, SLOTS, rows.shape[1])
        return lax.all_to_all(
            blocks, ("seq", "exp"), split_axis=0, concat_axis=0, tiled=True
        ).reshape(rows.shape)

    received = exchange(send)
    returned = exchange(expert(received, w_gate, w_up, w_down))
    return combine(returned, rank, weight, resid[0], projected)[None]


def solution(mesh):
    in_specs = (
        P("exp", "seq", None),
        P("exp", "seq", None),
        P("exp", "seq", None),
        P("exp", "seq", None),
        P("exp", None, "seq", None),
        P("exp", None, "seq", None),
        P("exp"),
        P("seq", None),
        P(),
        P(),
        P("exp", "seq", None),
        P(("seq", "exp"), None, None),
        P(("seq", "exp"), None, None),
        P(("seq", "exp"), None, None),
    )
    out_specs = P("exp", "seq", None)
    return jax.shard_map(
        per_device, mesh=mesh, in_specs=in_specs, out_specs=out_specs, check_vma=False
    )
```

```python
import functools

import jax
import jax.numpy as jnp
import numpy as np
from jax import lax
from jax.experimental import pallas as pl
from jax.experimental.pallas import tpu as pltpu
from jax.sharding import PartitionSpec as P

QUERY_HEAD_HALF = 32
KEY_VALUE_HEADS = 4
HEAD_SIZE = 128
TOP = 8
SLOTS = 8
EXTRA = 512
MIB = 1 << 20


def dot(a, b):
    return jnp.dot(a, b, preferred_element_type=jnp.float32)


def dot_nt(a, b):
    return lax.dot_general(a, b, (((1,), (1,)), ((), ())), preferred_element_type=jnp.float32)


def pack_kernel(query_ref, key_ref, value_ref, key_cache_ref, value_cache_ref, out_ref):
    cached = key_cache_ref.shape[2]
    lanes = query_ref.shape[2]
    out_ref[0, :, :lanes] = query_ref[0]
    out_ref[0, :, lanes : lanes + HEAD_SIZE] = key_ref[0]
    out_ref[0, :, lanes + HEAD_SIZE : lanes + 2 * HEAD_SIZE] = value_ref[0]
    out_ref[0, :cached, lanes + 2 * HEAD_SIZE :] = key_cache_ref[0, 0]
    out_ref[0, cached:, lanes + 2 * HEAD_SIZE :] = value_cache_ref[0, 0]


def pack(queries, keys, values, key_cache, value_cache, seq_count):
    tokens, width = queries.shape[1:]
    cached = key_cache.shape[2]
    assert 2 * cached == tokens
    lanes = width // seq_count
    sharers = seq_count // KEY_VALUE_HEADS
    cache_spec = pl.BlockSpec((1, 1, cached, HEAD_SIZE), lambda s: (0, s // sharers, 0, 0))
    head_spec = pl.BlockSpec((1, tokens, HEAD_SIZE), lambda s: (0, 0, s // sharers))
    return pl.pallas_call(
        pack_kernel,
        grid=(seq_count,),
        in_specs=[
            pl.BlockSpec((1, tokens, lanes), lambda s: (0, 0, s)),
            head_spec,
            head_spec,
            cache_spec,
            cache_spec,
        ],
        out_specs=pl.BlockSpec((1, tokens, lanes + 3 * HEAD_SIZE), lambda s: (s, 0, 0)),
        out_shape=jax.ShapeDtypeStruct(
            (seq_count, tokens, lanes + 3 * HEAD_SIZE), jnp.bfloat16
        ),
        name="pack",
    )(queries, keys, values, key_cache, value_cache)


def attend_kernel(length_ref, packed_ref, out_weight_ref, out_ref, key_ref, value_ref, att_ref):
    step = pl.program_id(0)
    parts, tokens, _ = packed_ref.shape
    lanes = out_weight_ref.shape[0]
    heads = lanes // HEAD_SIZE
    cached = tokens // 2
    prefix = parts * cached
    rows = out_ref.shape[0]
    per_step = rows // tokens
    rate = HEAD_SIZE ** (-0.5) * float(np.log2(np.e))

    @pl.when(step == 0)
    def _():
        for t in range(parts):
            old = pl.ds(t * cached, cached)
            new = pl.ds(prefix + t * tokens, tokens)
            key_ref[old, :] = packed_ref[t, :cached, lanes + 2 * HEAD_SIZE :]
            value_ref[old, :] = packed_ref[t, cached:, lanes + 2 * HEAD_SIZE :]
            key_ref[new, :] = packed_ref[t, :, lanes : lanes + HEAD_SIZE]
            value_ref[new, :] = packed_ref[t, :, lanes + HEAD_SIZE : lanes + 2 * HEAD_SIZE]

    in_prefix = lax.broadcasted_iota(jnp.int32, (rows, prefix), 1) < length_ref[0]
    causal = lax.broadcasted_iota(jnp.int32, (rows, rows), 1) <= lax.broadcasted_iota(
        jnp.int32, (rows, rows), 0
    )

    def block(i):
        spans = [(0, prefix)]
        if i:
            spans.append((prefix, i * rows))
        spans.append((prefix + i * rows, rows))
        for h in range(heads):
            query = jnp.concatenate(
                [
                    packed_ref[i * per_step + t, :, h * HEAD_SIZE : (h + 1) * HEAD_SIZE]
                    for t in range(per_step)
                ],
                axis=0,
            )
            scores = [dot_nt(query, key_ref[pl.ds(start, size), :]) for start, size in spans]
            scores[0] = jnp.where(in_prefix, scores[0], -1e30)
            scores[-1] = jnp.where(causal, scores[-1], -1e30)
            top = functools.reduce(
                jnp.maximum, [jnp.max(s, axis=1, keepdims=True) for s in scores]
            )
            total, result = 0.0, 0.0
            for s, (start, size) in zip(scores, spans, strict=True):
                raised = jnp.exp2((s - top) * rate)
                total = total + jnp.sum(raised, axis=1, keepdims=True)
                result = result + dot(
                    raised.astype(jnp.bfloat16), value_ref[pl.ds(start, size), :]
                )
            att_ref[:, h * HEAD_SIZE : (h + 1) * HEAD_SIZE] = (result / total).astype(
                jnp.bfloat16
            )

    for i in range(parts // per_step):
        pl.when(step == i)(functools.partial(block, i))
    out_ref[...] = dot(att_ref[...], out_weight_ref[...]).astype(jnp.bfloat16)


def attend(length, packed, out_weight, rows=256):
    parts, tokens, columns = packed.shape
    lanes, width = out_weight.shape
    span = parts * tokens
    total = span + parts * tokens // 2
    return pl.pallas_call(
        attend_kernel,
        grid=(span // rows,),
        in_specs=[
            pl.BlockSpec(memory_space=pltpu.SMEM),
            pl.BlockSpec((parts, tokens, columns), lambda i: (0, 0, 0)),
            pl.BlockSpec((lanes, width), lambda i: (0, 0)),
        ],
        out_specs=pl.BlockSpec((rows, width), lambda i: (i, 0)),
        out_shape=jax.ShapeDtypeStruct((span, width), jnp.bfloat16),
        scratch_shapes=[
            pltpu.VMEM((total, HEAD_SIZE), jnp.bfloat16),
            pltpu.VMEM((total, HEAD_SIZE), jnp.bfloat16),
            pltpu.VMEM((rows, lanes), jnp.bfloat16),
        ],
        compiler_params=pltpu.CompilerParams(vmem_limit_bytes=48 * MIB),
        name="attend",
    )(length, packed, out_weight)


def named_mask(ids_ref, experts):
    tokens = ids_ref.shape[0]
    lane = lax.broadcasted_iota(jnp.int32, (tokens, experts), 1)
    named = ids_ref[:, 0:1] == lane
    for k in range(1, TOP):
        named = named | (ids_ref[:, k : k + 1] == lane)
    return named


def flags(condition):
    return jnp.where(condition, 1.0, 0.0).astype(jnp.bfloat16)


def plan_kernel(ids_ref, rank_ref, pick_ref, ninth_ref):
    tokens, experts = rank_ref.shape
    named = named_mask(ids_ref, experts)
    earlier = flags(
        lax.broadcasted_iota(jnp.int32, (tokens, tokens), 0)
        > lax.broadcasted_iota(jnp.int32, (tokens, tokens), 1)
    )
    rank = jnp.where(named, dot(earlier, flags(named)) + 1.0, 0.0)
    rank_ref[...] = rank
    narrow = rank.astype(jnp.bfloat16)
    row = lax.broadcasted_iota(jnp.int32, (experts * SLOTS, experts), 0)
    spread = flags(row // SLOTS == lax.broadcasted_iota(jnp.int32, row.shape, 1))
    slot = (lax.broadcasted_iota(jnp.int32, (experts * SLOTS, tokens), 0) % SLOTS).astype(
        jnp.float32
    )
    pick_ref[...] = flags(dot_nt(spread, narrow) == slot + 1.0)
    same = flags(
        lax.broadcasted_iota(jnp.int32, (experts, experts), 0)
        == lax.broadcasted_iota(jnp.int32, (experts, experts), 1)
    )
    ninth_ref[...] = flags(dot_nt(same, narrow) == SLOTS + 1.0)


def plan(ids, experts):
    tokens = ids.shape[0]
    return pl.pallas_call(
        plan_kernel,
        out_shape=[
            jax.ShapeDtypeStruct((tokens, experts), jnp.float32),
            jax.ShapeDtypeStruct((experts * SLOTS, tokens), jnp.bfloat16),
            jax.ShapeDtypeStruct((experts, tokens), jnp.bfloat16),
        ],
        name="plan",
    )(ids)


def route_kernel(
    resid_ref, proj_ref, gain_ref, pick_ref, ninth_ref, send_ref, normed_ref, extra_ref
):
    step = pl.program_id(0)
    cols = send_ref.shape[1]
    blocks = resid_ref.shape[1] // cols
    experts = ninth_ref.shape[0]

    @pl.when(step == 0)
    def _():
        hidden = resid_ref[...].astype(jnp.float32) + proj_ref[...].astype(jnp.float32)
        mean_square = jnp.mean(hidden * hidden, axis=1, keepdims=True)
        normed_ref[...] = (
            hidden * lax.rsqrt(mean_square + 1e-06) * gain_ref[...]
        ).astype(jnp.bfloat16)

    for j in range(blocks):

        @pl.when(step == j)
        def _():
            part = normed_ref[:, j * cols : (j + 1) * cols]
            send_ref[...] = dot(pick_ref[...], part).astype(jnp.bfloat16)
            ninth = dot(ninth_ref[...], part)
            for a in range(cols // EXTRA):
                piece = j * (cols // EXTRA) + a
                for b in range(EXTRA // 128):
                    extra_ref[b, pl.ds(piece, experts, stride=SLOTS), :] = ninth[
                        :, a * EXTRA + b * 128 : a * EXTRA + (b + 1) * 128
                    ]

    @pl.when(step == blocks)
    def _():
        for b in range(EXTRA // 128):
            send_ref[:, b * 128 : (b + 1) * 128] = extra_ref[b].astype(jnp.bfloat16)


def route(resid, projected, gain, pick, ninth):
    tokens, width = resid.shape
    experts = ninth.shape[0]
    cols = width // SLOTS
    whole = lambda shape: pl.BlockSpec(shape, lambda j: (0, 0))
    return pl.pallas_call(
        route_kernel,
        grid=(SLOTS + 1,),
        in_specs=[
            whole((tokens, width)),
            whole((tokens, width)),
            whole((1, width)),
            whole(pick.shape),
            whole(ninth.shape),
        ],
        out_specs=[
            pl.BlockSpec((experts * SLOTS, cols), lambda j: (0, j)),
            whole((tokens, width)),
        ],
        out_shape=[
            jax.ShapeDtypeStruct((experts * SLOTS, width + cols), jnp.bfloat16),
            jax.ShapeDtypeStruct((tokens, width), jnp.bfloat16),
        ],
        scratch_shapes=[pltpu.VMEM((EXTRA // 128, experts * SLOTS, 128), jnp.float32)],
        compiler_params=pltpu.CompilerParams(vmem_limit_bytes=48 * MIB),
        name="route",
    )(resid, projected, gain, pick, ninth)


def weights_kernel(normed_ref, router_ref, rank_ref, main_ref, ninth_ref):
    tokens, experts = rank_ref.shape
    rank = rank_ref[...]
    named = rank > 0.0
    logits = dot(normed_ref[...], router_ref[...])
    top = jnp.max(jnp.where(named, logits, -jnp.inf), axis=1, keepdims=True)
    raised = jnp.where(named, jnp.exp(jnp.where(named, logits, top) - top), 0.0)
    weight = raised / jnp.sum(raised, axis=1, keepdims=True)
    high = weight.astype(jnp.bfloat16)
    low = (weight - high.astype(jnp.float32)).astype(jnp.bfloat16)
    column = lax.broadcasted_iota(jnp.int32, (experts, experts * SLOTS), 1)
    spread = flags(column // SLOTS == lax.broadcasted_iota(jnp.int32, column.shape, 0))
    wide_rank = dot(rank.astype(jnp.bfloat16), spread)
    slot = (lax.broadcasted_iota(jnp.int32, wide_rank.shape, 1) % SLOTS).astype(jnp.float32)
    for half, part in enumerate((high, low)):
        rows = pl.ds(half * tokens, tokens)
        main_ref[rows, :] = jnp.where(wide_rank == slot + 1.0, dot(part, spread), 0.0).astype(
            jnp.bfloat16
        )
        ninth_ref[rows, :] = jnp.where(
            rank == SLOTS + 1.0, part.astype(jnp.float32), 0.0
        ).astype(jnp.bfloat16)


def weights(normed, router, rank):
    tokens, experts = rank.shape
    return pl.pallas_call(
        weights_kernel,
        out_shape=[
            jax.ShapeDtypeStruct((2 * tokens, experts * SLOTS), jnp.bfloat16),
            jax.ShapeDtypeStruct((2 * tokens, experts), jnp.bfloat16),
        ],
        compiler_params=pltpu.CompilerParams(vmem_limit_bytes=32 * MIB),
        name="weights",
    )(normed, router, rank)


def expert_kernel(
    rows_ref, extra_ref, gate_ref, up_ref, *refs, deep, wide
):
    down_refs, (out_ref, ninth_ref, gate_acc, up_acc, act_ref, piece_ref) = (
        refs[:wide],
        refs[wide:],
    )
    step = pl.program_id(0)
    main, cols = rows_ref.shape
    sources = main // SLOTS

    @pl.when(step == 0)
    def _():
        for b in range(EXTRA // 128):
            piece_ref[b] = extra_ref[:, b * 128 : (b + 1) * 128].astype(jnp.float32)
        for j in range(SLOTS):
            for b in range(EXTRA // 128):
                lane = (j * EXTRA + b * 128) % cols
                ninth_ref[(j * EXTRA) // cols, :, lane : lane + 128] = piece_ref[
                    b, pl.ds(j, sources, stride=SLOTS), :
                ].astype(jnp.bfloat16)

    @pl.when(step < deep)
    def _():
        ninth = ninth_ref[jnp.minimum(step, deep - 1)]
        rows = jnp.concatenate([rows_ref[...], ninth], axis=0)

        @pl.when(step == 0)
        def _():
            gate_acc[...] = dot(rows, gate_ref[0])
            up_acc[...] = dot(rows, up_ref[0])

        @pl.when(step > 0)
        def _():
            gate_acc[...] += dot(rows, gate_ref[0])
            up_acc[...] += dot(rows, up_ref[0])

    @pl.when(step == deep - 1)
    def _():
        gate_val = gate_acc[...]
        act_ref[...] = (gate_val / (1.0 + jnp.exp(-gate_val)) * up_acc[...]).astype(jnp.bfloat16)

    last = (SLOTS + 1) // wide
    for s in range(last):

        @pl.when(step == deep + s)
        def _():
            for a in range(wide):
                j = s * wide + a
                lanes = slice(a * EXTRA, (a + 1) * EXTRA)
                if j < SLOTS:
                    result = dot(act_ref[...], down_refs[a][0])
                    out_ref[:, lanes] = result[:main].astype(jnp.bfloat16)
                    for b in range(EXTRA // 128):
                        piece_ref[b, pl.ds(j, sources, stride=SLOTS), :] = result[
                            main:, b * 128 : (b + 1) * 128
                        ]
                else:
                    for b in range(EXTRA // 128):
                        out_ref[:, a * EXTRA + b * 128 : a * EXTRA + (b + 1) * 128] = piece_ref[
                            b
                        ].astype(jnp.bfloat16)


def expert(rows, w_gate, w_up, w_down, deep=4, wide=3):
    main = rows.shape[0]
    _, width, hidden = w_gate.shape
    cols = width // deep
    tall = main + main // SLOTS
    last = (SLOTS + 1) // wide
    first = lambda s: jnp.minimum(s, deep - 1)

    def down_spec(a):
        return pl.BlockSpec(
            (1, hidden, EXTRA),
            lambda s: (0, 0, jnp.minimum(jnp.clip(s - deep, 0, last - 1) * wide + a, SLOTS - 1)),
        )

    return pl.pallas_call(
        functools.partial(expert_kernel, deep=deep, wide=wide),
        grid=(deep + last,),
        in_specs=[
            pl.BlockSpec((main, cols), lambda s: (0, first(s))),
            pl.BlockSpec((main, EXTRA), lambda s: (0, SLOTS)),
            pl.BlockSpec((1, cols, hidden), lambda s: (0, first(s), 0)),
            pl.BlockSpec((1, cols, hidden), lambda s: (0, first(s), 0)),
            *[down_spec(a) for a in range(wide)],
        ],
        out_specs=pl.BlockSpec((main, wide * EXTRA), lambda s: (0, jnp.clip(s - deep, 0, last - 1))),
        out_shape=jax.ShapeDtypeStruct(rows.shape, jnp.bfloat16),
        scratch_shapes=[
            pltpu.VMEM((deep, main // SLOTS, cols), jnp.bfloat16),
            pltpu.VMEM((tall, hidden), jnp.float32),
            pltpu.VMEM((tall, hidden), jnp.float32),
            pltpu.VMEM((tall, hidden), jnp.bfloat16),
            pltpu.VMEM((EXTRA // 128, main, 128), jnp.float32),
        ],
        compiler_params=pltpu.CompilerParams(vmem_limit_bytes=56 * MIB),
        name="expert",
    )(rows, rows, w_gate, w_up, *[w_down] * wide)


def combine_kernel(
    rows_ref, extra_ref, main_ref, ninth_ref, resid_ref, proj_ref, out_ref, piece_ref, row_ref
):
    step = pl.program_id(0)
    tokens = resid_ref.shape[0]
    sources = rows_ref.shape[0] // SLOTS

    @pl.when(step == 0)
    def _():
        for b in range(EXTRA // 128):
            piece_ref[b] = extra_ref[:, b * 128 : (b + 1) * 128].astype(jnp.float32)
        for j in range(SLOTS):
            for b in range(EXTRA // 128):
                row_ref[j, :, b * 128 : (b + 1) * 128] = piece_ref[
                    b, pl.ds(j, sources, stride=SLOTS), :
                ].astype(jnp.bfloat16)

    both = dot(main_ref[...], rows_ref[...]) + dot(ninth_ref[...], row_ref[step])
    hidden = resid_ref[...].astype(jnp.float32) + proj_ref[...].astype(jnp.float32)
    out_ref[...] = (hidden + (both[:tokens] + both[tokens:])).astype(jnp.bfloat16)


def combine(rows, main_weight, ninth_weight, resid, projected):
    tokens, width = resid.shape
    main = rows.shape[0]
    cols = width // SLOTS
    whole = lambda shape: pl.BlockSpec(shape, lambda j: (0, 0))
    part = pl.BlockSpec((tokens, cols), lambda j: (0, j))
    return pl.pallas_call(
        combine_kernel,
        grid=(SLOTS,),
        in_specs=[
            pl.BlockSpec((main, cols), lambda j: (0, j)),
            pl.BlockSpec((main, cols), lambda j: (0, SLOTS)),
            whole(main_weight.shape),
            whole(ninth_weight.shape),
            part,
            part,
        ],
        out_specs=part,
        out_shape=jax.ShapeDtypeStruct((tokens, width), jnp.bfloat16),
        scratch_shapes=[
            pltpu.VMEM((EXTRA // 128, main, 128), jnp.float32),
            pltpu.VMEM((SLOTS, main // SLOTS, cols), jnp.bfloat16),
        ],
        compiler_params=pltpu.CompilerParams(vmem_limit_bytes=48 * MIB),
        name="combine",
    )(rows, rows, main_weight, ninth_weight, resid, projected)


def per_device(
    resid,
    queries,
    span_rotated_keys,
    span_value_rows,
    key_cache,
    prefix_value_cache,
    prefix_len,
    out_weight,
    norm_gain,
    router_weight,
    expert_ids,
    w_gate,
    w_up,
    w_down,
):
    seq_count = lax.axis_size("seq")
    width = resid.shape[2]
    experts = router_weight.shape[1]
    packed = pack(
        queries, span_rotated_keys, span_value_rows, key_cache, prefix_value_cache, seq_count
    )
    packed = lax.all_to_all(packed, "seq", split_axis=0, concat_axis=0, tiled=True)
    projected = lax.psum_scatter(
        attend(prefix_len, packed, out_weight), "seq", scatter_dimension=0, tiled=True
    )
    rank, pick, ninth = plan(expert_ids[0], experts)
    send, normed = route(resid[0], projected, norm_gain.reshape(1, width), pick, ninth)

    def exchange(rows):
        blocks = rows.reshape(experts, SLOTS, rows.shape[1])
        return lax.all_to_all(
            blocks, ("seq", "exp"), split_axis=0, concat_axis=0, tiled=True
        ).reshape(rows.shape)

    received = exchange(send)
    main_weight, ninth_weight = weights(normed, router_weight, rank)
    returned = exchange(expert(received, w_gate, w_up, w_down))
    return combine(returned, main_weight, ninth_weight, resid[0], projected)[None]


def solution(mesh):
    in_specs = (
        P("exp", "seq", None),
        P("exp", "seq", None),
        P("exp", "seq", None),
        P("exp", "seq", None),
        P("exp", None, "seq", None),
        P("exp", None, "seq", None),
        P("exp"),
        P("seq", None),
        P(),
        P(),
        P("exp", "seq", None),
        P(("seq", "exp"), None, None),
        P(("seq", "exp"), None, None),
        P(("seq", "exp"), None, None),
    )
    out_specs = P("exp", "seq", None)
    return jax.shard_map(
        per_device, mesh=mesh, in_specs=in_specs, out_specs=out_specs, check_vma=False
    )
```

```python
import functools

import jax
import jax.numpy as jnp
import numpy as np
from jax import lax
from jax.experimental import pallas as pl
from jax.experimental.pallas import tpu as pltpu
from jax.sharding import PartitionSpec as P

QUERY_HEAD_HALF = 32
KEY_VALUE_HEADS = 4
HEAD_SIZE = 128
TOP = 8
SLOTS = 8
HALF = SLOTS // 2
GROUP = 256
MIB = 1 << 20


def dot(a, b):
    return jnp.dot(a, b, preferred_element_type=jnp.float32)


def in_hbm(x):
    return pltpu.with_memory_space_constraint(x, pltpu.HBM)


def dot_nt(a, b):
    return lax.dot_general(a, b, (((1,), (1,)), ((), ())), preferred_element_type=jnp.float32)


def pack_kernel(query_ref, key_ref, value_ref, key_cache_ref, value_cache_ref, out_ref, sems):
    parts = out_ref.shape[0]
    cached, tokens = key_cache_ref.shape[2], query_ref.shape[1]
    lanes = query_ref.shape[2] // parts
    ends = [lanes + i * HEAD_SIZE for i in range(4)]
    copies = []
    for s in range(parts):
        head = s * KEY_VALUE_HEADS // parts
        heads = pl.ds(head * HEAD_SIZE, HEAD_SIZE)
        moves = [
            (query_ref.at[0, :, pl.ds(s * lanes, lanes)], out_ref.at[s, :, pl.ds(0, lanes)]),
            (key_ref.at[0, :, heads], out_ref.at[s, :, pl.ds(ends[0], HEAD_SIZE)]),
            (value_ref.at[0, :, heads], out_ref.at[s, :, pl.ds(ends[1], HEAD_SIZE)]),
            (
                key_cache_ref.at[0, head],
                out_ref.at[s, pl.ds(0, cached), pl.ds(ends[2], HEAD_SIZE)],
            ),
            (
                value_cache_ref.at[0, head],
                out_ref.at[s, pl.ds(cached, tokens - cached), pl.ds(ends[2], HEAD_SIZE)],
            ),
        ]
        for i, (source, target) in enumerate(moves):
            copies.append(pltpu.make_async_copy(source, target, sems.at[s, i]))
    for copy in copies:
        copy.start()
    for copy in copies:
        copy.wait()


def pack(queries, keys, values, key_cache, value_cache, seq_count):
    tokens, width = queries.shape[1:]
    cached = key_cache.shape[2]
    assert 2 * cached == tokens
    lanes = width // seq_count
    return pl.pallas_call(
        pack_kernel,
        in_specs=[pl.BlockSpec(memory_space=pltpu.HBM)] * 5,
        out_specs=pl.BlockSpec(memory_space=pltpu.HBM),
        out_shape=jax.ShapeDtypeStruct(
            (seq_count, tokens, lanes + 3 * HEAD_SIZE), jnp.bfloat16
        ),
        scratch_shapes=[pltpu.SemaphoreType.DMA((seq_count, 5))],
        name="pack",
    )(queries, keys, values, key_cache, value_cache)


def attend_kernel(
    length_ref, packed_ref, out_weight_hbm, out_ref,
    key_ref, value_ref, att_ref, out_weight_ref, sem,
):
    step = pl.program_id(0)
    parts, tokens, _ = packed_ref.shape
    lanes = out_weight_ref.shape[0]
    heads = lanes // HEAD_SIZE
    cached = tokens // 2
    prefix = parts * cached
    rows = out_ref.shape[0]
    per_step = rows // tokens
    rate = HEAD_SIZE ** (-0.5) * float(np.log2(np.e))
    fetch = pltpu.make_async_copy(out_weight_hbm, out_weight_ref, sem)

    @pl.when(step == 0)
    def _():
        fetch.start()
        for t in range(parts):
            old = pl.ds(t * cached, cached)
            new = pl.ds(prefix + t * tokens, tokens)
            key_ref[old, :] = packed_ref[t, :cached, lanes + 2 * HEAD_SIZE :]
            value_ref[old, :] = packed_ref[t, cached:, lanes + 2 * HEAD_SIZE :]
            key_ref[new, :] = packed_ref[t, :, lanes : lanes + HEAD_SIZE]
            value_ref[new, :] = packed_ref[t, :, lanes + HEAD_SIZE : lanes + 2 * HEAD_SIZE]

    in_prefix = lax.broadcasted_iota(jnp.int32, (rows, prefix), 1) < length_ref[0]
    causal = lax.broadcasted_iota(jnp.int32, (rows, rows), 1) <= lax.broadcasted_iota(
        jnp.int32, (rows, rows), 0
    )

    def block(i):
        spans = [(0, prefix)]
        if i:
            spans.append((prefix, i * rows))
        spans.append((prefix + i * rows, rows))
        for h in range(heads):
            query = jnp.concatenate(
                [
                    packed_ref[i * per_step + t, :, h * HEAD_SIZE : (h + 1) * HEAD_SIZE]
                    for t in range(per_step)
                ],
                axis=0,
            )
            scores = [dot_nt(query, key_ref[pl.ds(start, size), :]) for start, size in spans]
            scores[0] = jnp.where(in_prefix, scores[0], -1e30)
            scores[-1] = jnp.where(causal, scores[-1], -1e30)
            top = functools.reduce(
                jnp.maximum, [jnp.max(s, axis=1, keepdims=True) for s in scores]
            )
            total, result = 0.0, 0.0
            for s, (start, size) in zip(scores, spans, strict=True):
                raised = jnp.exp2((s - top) * rate)
                total = total + jnp.sum(raised, axis=1, keepdims=True)
                result = result + dot(
                    raised.astype(jnp.bfloat16), value_ref[pl.ds(start, size), :]
                )
            att_ref[:, h * HEAD_SIZE : (h + 1) * HEAD_SIZE] = (result / total).astype(
                jnp.bfloat16
            )

    for i in range(parts // per_step):
        pl.when(step == i)(functools.partial(block, i))
    pl.when(step == 0)(fetch.wait)
    out_ref[...] = dot(att_ref[...], out_weight_ref[...]).astype(jnp.bfloat16)


def attend(length, packed, out_weight, rows=256):
    parts, tokens, columns = packed.shape
    lanes, width = out_weight.shape
    span = parts * tokens
    total = span + parts * tokens // 2
    return pl.pallas_call(
        attend_kernel,
        grid=(span // rows,),
        in_specs=[
            pl.BlockSpec(memory_space=pltpu.SMEM),
            pl.BlockSpec((parts, tokens, columns), lambda i: (0, 0, 0)),
            pl.BlockSpec(memory_space=pltpu.HBM),
        ],
        out_specs=pl.BlockSpec((rows, width), lambda i: (i, 0)),
        out_shape=jax.ShapeDtypeStruct((span, width), jnp.bfloat16),
        scratch_shapes=[
            pltpu.VMEM((total, HEAD_SIZE), jnp.bfloat16),
            pltpu.VMEM((total, HEAD_SIZE), jnp.bfloat16),
            pltpu.VMEM((rows, lanes), jnp.bfloat16),
            pltpu.VMEM((lanes, width), jnp.bfloat16),
            pltpu.SemaphoreType.DMA,
        ],
        compiler_params=pltpu.CompilerParams(vmem_limit_bytes=48 * MIB),
        name="attend",
    )(length, packed, out_weight)


def named_mask(ids_ref, experts):
    tokens = ids_ref.shape[0]
    lane = lax.broadcasted_iota(jnp.int32, (tokens, experts), 1)
    named = ids_ref[:, 0:1] == lane
    for k in range(1, TOP):
        named = named | (ids_ref[:, k : k + 1] == lane)
    return named


def flags(condition):
    return jnp.where(condition, 1.0, 0.0).astype(jnp.bfloat16)


def spread_flags(experts, axis):
    shape = (experts * SLOTS, experts) if axis == 0 else (experts, experts * SLOTS)
    owner = lax.broadcasted_iota(jnp.int32, shape, axis) // SLOTS
    return flags(owner == lax.broadcasted_iota(jnp.int32, shape, 1 - axis))


def plan_kernel(ids_ref, rank_ref, pick_ref, ninth_ref):
    tokens, experts = rank_ref.shape
    named = named_mask(ids_ref, experts)
    earlier = flags(
        lax.broadcasted_iota(jnp.int32, (tokens, tokens), 0)
        > lax.broadcasted_iota(jnp.int32, (tokens, tokens), 1)
    )
    rank = jnp.where(named, dot(earlier, flags(named)) + 1.0, 0.0)
    rank_ref[...] = rank
    narrow = rank.astype(jnp.bfloat16)
    wide = dot_nt(spread_flags(experts, 0), narrow)
    row = lax.broadcasted_iota(jnp.int32, wide.shape, 0) % SLOTS
    slot = (row % HALF).astype(jnp.float32)
    for chunk in range(2):
        hit = wide == slot + float(1 + HALF * chunk)
        pick_ref[chunk, :, :tokens] = flags(hit & (row < HALF))
        pick_ref[chunk, :, tokens:] = flags(hit & (row >= HALF))
    same = flags(
        lax.broadcasted_iota(jnp.int32, (experts, experts), 0)
        == lax.broadcasted_iota(jnp.int32, (experts, experts), 1)
    )
    ninth_ref[...] = flags(dot_nt(same, narrow) == SLOTS + 1.0)


def plan(ids, experts):
    tokens = ids.shape[0]
    return pl.pallas_call(
        plan_kernel,
        out_shape=[
            pltpu.HBM((tokens, experts), jnp.float32),
            pltpu.HBM((2, experts * SLOTS, 2 * tokens), jnp.bfloat16),
            pltpu.HBM((experts, tokens), jnp.bfloat16),
        ],
        name="plan",
    )(ids)


def route_first_kernel(resid_ref, proj_ref, gain_ref, pick_ref, send_ref, halves_ref):
    step = pl.program_id(0)
    tokens, width = resid_ref.shape
    cols = send_ref.shape[1]
    half = width // 2

    @pl.when(step == 0)
    def _():
        hidden = resid_ref[...].astype(jnp.float32) + proj_ref[...].astype(jnp.float32)
        mean_square = jnp.mean(hidden * hidden, axis=1, keepdims=True)
        normed = (hidden * lax.rsqrt(mean_square + 1e-06) * gain_ref[...]).astype(jnp.bfloat16)
        halves_ref[:tokens, :] = normed[:, :half]
        halves_ref[tokens:, :] = normed[:, half:]

    for j in range(half // cols):

        @pl.when(step == j)
        def _():
            send_ref[...] = dot(
                pick_ref[0], halves_ref[:, j * cols : (j + 1) * cols]
            ).astype(jnp.bfloat16)


def route_first(resid, projected, gain, pick, cols=512):
    tokens, width = resid.shape
    rows, twice = pick.shape[1:]
    half = width // 2
    whole = lambda shape: pl.BlockSpec(shape, lambda j: (0,) * len(shape))
    return pl.pallas_call(
        route_first_kernel,
        grid=(half // cols,),
        in_specs=[
            whole((tokens, width)),
            whole((tokens, width)),
            whole((1, width)),
            whole((1, rows, twice)),
        ],
        out_specs=[pl.BlockSpec((rows, cols), lambda j: (0, j)), whole((twice, half))],
        out_shape=[
            pltpu.HBM((rows, half), jnp.bfloat16),
            pltpu.HBM((twice, half), jnp.bfloat16),
        ],
        compiler_params=pltpu.CompilerParams(vmem_limit_bytes=32 * MIB),
        name="route_first",
    )(resid, projected, gain, pick)


def route_second_kernel(halves_ref, pick_ref, ninth_ref, send_ref, extra_ref):
    step = pl.program_id(0)
    twice, half = halves_ref.shape
    cols = send_ref.shape[1]
    experts, tokens = ninth_ref.shape
    steps = half // cols

    for j in range(steps):

        @pl.when(step == j)
        def _():
            part = halves_ref[:, j * cols : (j + 1) * cols]
            send_ref[...] = dot(pick_ref[0], part).astype(jnp.bfloat16)
            for side in range(2):
                piece = dot(ninth_ref[...], part[side * tokens : (side + 1) * tokens])
                for b in range(cols // 128):
                    extra_ref[b, pl.ds(side * steps + j, experts, stride=SLOTS), :] = piece[
                        :, b * 128 : (b + 1) * 128
                    ]

    @pl.when(step == steps)
    def _():
        for b in range(cols // 128):
            send_ref[:, b * 128 : (b + 1) * 128] = extra_ref[b].astype(jnp.bfloat16)


def route_second(halves, pick, ninth):
    twice, half = halves.shape
    rows = pick.shape[1]
    cols = 2 * half // SLOTS
    whole = lambda shape: pl.BlockSpec(shape, lambda j: (0,) * len(shape))
    return pl.pallas_call(
        route_second_kernel,
        grid=(half // cols + 1,),
        in_specs=[
            whole((twice, half)),
            pl.BlockSpec((1, rows, twice), lambda j: (1, 0, 0)),
            whole(ninth.shape),
        ],
        out_specs=pl.BlockSpec((rows, cols), lambda j: (0, j)),
        out_shape=pltpu.HBM((rows, half + cols), jnp.bfloat16),
        scratch_shapes=[pltpu.VMEM((cols // 128, rows, 128), jnp.float32)],
        compiler_params=pltpu.CompilerParams(vmem_limit_bytes=32 * MIB),
        name="route_second",
    )(halves, pick, ninth)


def weights_kernel(halves_ref, router_ref, rank_ref, main_ref, ninth_ref):
    tokens, experts = rank_ref.shape
    half = halves_ref.shape[1]
    rank = rank_ref[...]
    named = rank > 0.0
    logits = dot(halves_ref[:tokens, :], router_ref[:half, :]) + dot(
        halves_ref[tokens:, :], router_ref[half:, :]
    )
    top = jnp.max(jnp.where(named, logits, -jnp.inf), axis=1, keepdims=True)
    raised = jnp.where(named, jnp.exp(jnp.where(named, logits, top) - top), 0.0)
    weight = raised / jnp.sum(raised, axis=1, keepdims=True)
    high = weight.astype(jnp.bfloat16)
    low = (weight - high.astype(jnp.float32)).astype(jnp.bfloat16)
    spread = spread_flags(experts, 1)
    wide_rank = dot(rank.astype(jnp.bfloat16), spread)
    row = lax.broadcasted_iota(jnp.int32, wide_rank.shape, 1) % SLOTS
    slot = (row % HALF).astype(jnp.float32)
    for term, part in enumerate((high, low)):
        place = pl.ds(term * tokens, tokens)
        wide = dot(part, spread)
        for chunk in range(2):
            kept = jnp.where(wide_rank == slot + float(1 + HALF * chunk), wide, 0.0)
            main_ref[chunk, 0, place, :] = jnp.where(row < HALF, kept, 0.0).astype(jnp.bfloat16)
            main_ref[chunk, 1, place, :] = jnp.where(row >= HALF, kept, 0.0).astype(jnp.bfloat16)
        ninth_ref[place, :] = jnp.where(
            rank == SLOTS + 1.0, part.astype(jnp.float32), 0.0
        ).astype(jnp.bfloat16)


def weights(halves, router, rank):
    tokens, experts = rank.shape
    return pl.pallas_call(
        weights_kernel,
        out_shape=[
            pltpu.HBM((2, 2, 2 * tokens, experts * SLOTS), jnp.bfloat16),
            pltpu.HBM((2 * tokens, experts), jnp.bfloat16),
        ],
        compiler_params=pltpu.CompilerParams(vmem_limit_bytes=32 * MIB),
        name="weights",
    )(halves, router, rank)


def sort_rows():
    to = lax.broadcasted_iota(jnp.int32, (GROUP, GROUP), 0)
    source = lax.broadcasted_iota(jnp.int32, (GROUP, GROUP), 1)
    count = GROUP // 2
    side, index = to // count, to % count
    return flags(source == index // HALF * SLOTS + side * HALF + index % HALF)


def sort_pieces():
    to = lax.broadcasted_iota(jnp.int32, (GROUP, GROUP), 0)
    source = lax.broadcasted_iota(jnp.int32, (GROUP, GROUP), 1)
    count = GROUP // SLOTS
    return flags(source == to % count * SLOTS + to // count)


def dot_tn(a, b):
    return lax.dot_general(a, b, (((0,), (0,)), ((), ())), preferred_element_type=jnp.float32)


def expert_kernel(*refs, deep, ninth):
    rows_ref, refs = refs[0], refs[1:]
    gate_ref, up_ref, first_ref, second_ref, out_ref = refs[:5]
    token_ref, gate_acc, up_acc, act_ref, piece_ref = refs[5:]
    step = pl.program_id(0)
    groups = out_ref.shape[0] // GROUP
    count = GROUP // 2
    few = GROUP // SLOTS
    main = groups * count
    cols = out_ref.shape[1]
    half = rows_ref.shape[1] - (cols if ninth else 0)
    deep_cols = gate_ref.shape[1]
    steps = half // cols

    @pl.when(step < groups)
    def _():
        g = jnp.minimum(step, groups - 1)
        place = pl.ds(pl.multiple_of(g * count, count), count)
        lined = dot(sort_rows(), rows_ref[:, :half]).astype(jnp.bfloat16)
        for k in range(deep):
            side, lane = divmod(k * deep_cols, half)
            token_ref[k, place, :] = lined[
                side * count : (side + 1) * count, lane : lane + deep_cols
            ]
        if ninth:
            place = pl.ds(pl.multiple_of(main + g * few, few), few)
            pieces = dot(sort_pieces(), rows_ref[:, half:]).astype(jnp.bfloat16)
            for j in range(SLOTS):
                k, lane = divmod(j * cols, deep_cols)
                token_ref[k, place, lane : lane + cols] = pieces[j * few : (j + 1) * few]

    start = groups

    @pl.when(step == start)
    def _():
        gate_acc[...] = dot(token_ref[0], gate_ref[0])
        up_acc[...] = dot(token_ref[0], up_ref[0])

    @pl.when((step > start) & (step < start + deep))
    def _():
        rows = token_ref[jnp.clip(step - start, 0, deep - 1)]
        gate_acc[...] += dot(rows, gate_ref[0])
        up_acc[...] += dot(rows, up_ref[0])

    @pl.when(step == start + deep - 1)
    def _():
        gate_val = gate_acc[...]
        act_ref[...] = (gate_val / (1.0 + jnp.exp(-gate_val)) * up_acc[...]).astype(jnp.bfloat16)

    start = groups + deep

    @pl.when((step >= start) & (step < start + steps))
    def _():
        act = act_ref[...]
        sides = [dot(act, ref[0]).astype(jnp.bfloat16) for ref in (first_ref, second_ref)]
        order = sort_rows()
        for g in range(groups):
            part = jnp.concatenate([side[g * count : (g + 1) * count] for side in sides], axis=0)
            out_ref[g * GROUP : (g + 1) * GROUP, :] = dot_tn(order, part).astype(jnp.bfloat16)
        if ninth:
            j = jnp.clip(step - start, 0, steps - 1)
            for which, side in enumerate(sides):
                piece_ref[j + which * steps] = side[main:]

    if ninth:

        @pl.when(step == start + steps)
        def _():
            order = sort_pieces()
            for g in range(groups):
                part = jnp.concatenate(
                    [piece_ref[j, g * few : (g + 1) * few, :] for j in range(SLOTS)], axis=0
                )
                out_ref[g * GROUP : (g + 1) * GROUP, :] = dot_tn(order, part).astype(jnp.bfloat16)


def expert(rows, w_gate, w_up, w_down, ninth, deep=4):
    tall, columns = rows.shape
    _, width, hidden = w_gate.shape
    half, cols = width // 2, width // SLOTS
    assert columns == half + (cols if ninth else 0) and tall % GROUP == 0
    groups, steps = tall // GROUP, half // cols
    main = tall // 2 + (tall // SLOTS if ninth else 0)
    at = groups + deep
    inner = lambda s, begin, count: jnp.clip(s - begin, 0, count - 1)
    weight = pl.BlockSpec((1, width // deep, hidden), lambda s: (0, inner(s, groups, deep), 0))
    return pl.pallas_call(
        functools.partial(expert_kernel, deep=deep, ninth=ninth),
        grid=(at + steps + ninth,),
        in_specs=[
            pl.BlockSpec((GROUP, columns), lambda s: (inner(s, 0, groups), 0)),
            weight,
            weight,
            pl.BlockSpec((1, hidden, cols), lambda s: (0, 0, inner(s, at, steps))),
            pl.BlockSpec((1, hidden, cols), lambda s: (0, 0, steps + inner(s, at, steps))),
        ],
        out_specs=pl.BlockSpec((tall, cols), lambda s: (0, inner(s, at, steps + ninth))),
        out_shape=pltpu.HBM(rows.shape, jnp.bfloat16),
        scratch_shapes=[
            pltpu.VMEM((deep, main, width // deep), jnp.bfloat16),
            pltpu.VMEM((main, hidden), jnp.float32),
            pltpu.VMEM((main, hidden), jnp.float32),
            pltpu.VMEM((main, hidden), jnp.bfloat16),
            pltpu.VMEM((SLOTS, tall // SLOTS, cols), jnp.bfloat16),
        ],
        compiler_params=pltpu.CompilerParams(vmem_limit_bytes=40 * MIB),
        name="expert_second" if ninth else "expert_first",
    )(rows, w_gate, w_up, w_down, w_down)


def combine_first_kernel(rows_ref, weight_ref, *refs):
    resids, projs, outs = refs[:2], refs[2:4], refs[4:]
    tokens = outs[0].shape[0]
    for side in range(2):
        both = dot(weight_ref[0, side], rows_ref[...])
        hidden = resids[side][...].astype(jnp.float32) + projs[side][...].astype(jnp.float32)
        outs[side][...] = hidden + (both[:tokens] + both[tokens:])


def combine_first(rows, main_weight, resid, projected):
    tokens, width = resid.shape
    tall, half = rows.shape
    cols = width // SLOTS
    steps = half // cols
    first = pl.BlockSpec((tokens, cols), lambda j: (0, j))
    second = pl.BlockSpec((tokens, cols), lambda j: (0, steps + j))
    shape = pltpu.HBM((tokens, half), jnp.float32)
    return pl.pallas_call(
        combine_first_kernel,
        grid=(steps,),
        in_specs=[
            pl.BlockSpec((tall, cols), lambda j: (0, j)),
            pl.BlockSpec((1,) + main_weight.shape[1:], lambda j: (0, 0, 0, 0)),
            first,
            second,
            first,
            second,
        ],
        out_specs=[first, first],
        out_shape=[shape, shape],
        compiler_params=pltpu.CompilerParams(vmem_limit_bytes=32 * MIB),
        name="combine_first",
    )(rows, main_weight, resid, resid, projected, projected)


def combine_second_kernel(
    rows_ref, extra_ref, weight_ref, ninth_ref, first_ref, second_ref, out_ref, piece_ref
):
    step = pl.program_id(0)
    tall, cols = rows_ref.shape
    tokens = out_ref.shape[0]
    groups, few = tall // GROUP, GROUP // SLOTS
    steps = SLOTS // 2

    @pl.when(step == 0)
    def _():
        order = sort_pieces()
        for g in range(groups):
            pieces = dot(order, extra_ref[g * GROUP : (g + 1) * GROUP, :]).astype(jnp.bfloat16)
            for j in range(SLOTS):
                piece_ref[j, g * few : (g + 1) * few, :] = pieces[j * few : (j + 1) * few]

    for j in range(steps):

        @pl.when(step == j)
        def _():
            for side, ref in enumerate((first_ref, second_ref)):
                piece = side * steps + j
                both = dot(weight_ref[0, side], rows_ref[...]) + dot(
                    ninth_ref[...], piece_ref[piece]
                )
                out_ref[:, piece * cols : (piece + 1) * cols] = (
                    ref[...] + (both[:tokens] + both[tokens:])
                ).astype(jnp.bfloat16)


def combine_second(rows, main_weight, ninth_weight, first, second):
    tokens, half = first.shape
    tall = rows.shape[0]
    cols = 2 * half // SLOTS
    steps = half // cols
    part = pl.BlockSpec((tokens, cols), lambda j: (0, j))
    return pl.pallas_call(
        combine_second_kernel,
        grid=(steps,),
        in_specs=[
            pl.BlockSpec((tall, cols), lambda j: (0, j)),
            pl.BlockSpec((tall, cols), lambda j: (0, steps)),
            pl.BlockSpec((1,) + main_weight.shape[1:], lambda j: (1, 0, 0, 0)),
            pl.BlockSpec(ninth_weight.shape, lambda j: (0, 0)),
            part,
            part,
        ],
        out_specs=pl.BlockSpec((tokens, 2 * half), lambda j: (0, 0)),
        out_shape=jax.ShapeDtypeStruct((tokens, 2 * half), jnp.bfloat16),
        scratch_shapes=[pltpu.VMEM((SLOTS, tall // SLOTS, cols), jnp.bfloat16)],
        compiler_params=pltpu.CompilerParams(vmem_limit_bytes=32 * MIB),
        name="combine_second",
    )(rows, rows, main_weight, ninth_weight, first, second)


def per_device(
    resid,
    queries,
    span_rotated_keys,
    span_value_rows,
    key_cache,
    prefix_value_cache,
    prefix_len,
    out_weight,
    norm_gain,
    router_weight,
    expert_ids,
    w_gate,
    w_up,
    w_down,
):
    seq_count = lax.axis_size("seq")
    width = resid.shape[2]
    experts = router_weight.shape[1]
    packed = pack(
        queries, span_rotated_keys, span_value_rows, key_cache, prefix_value_cache, seq_count
    )
    packed = lax.all_to_all(packed, "seq", split_axis=0, concat_axis=0, tiled=True)
    projected = lax.psum_scatter(
        attend(prefix_len, packed, in_hbm(out_weight)), "seq", scatter_dimension=0, tiled=True
    )
    projected = in_hbm(projected)
    rank, pick, ninth = [in_hbm(x) for x in plan(expert_ids[0], experts)]
    send_first, halves = route_first(resid[0], projected, norm_gain.reshape(1, width), pick)

    def exchange(rows):
        blocks = rows.reshape(experts, SLOTS, rows.shape[1])
        return in_hbm(
            lax.all_to_all(
                blocks, ("seq", "exp"), split_axis=0, concat_axis=0, tiled=True
            ).reshape(rows.shape)
        )

    halves = in_hbm(halves)
    w_gate, w_up, w_down = in_hbm(w_gate), in_hbm(w_up), in_hbm(w_down)
    got_first = exchange(send_first)
    got_second = exchange(route_second(halves, pick, ninth))
    main_weight, ninth_weight = [in_hbm(x) for x in weights(halves, router_weight, rank)]
    back_first = exchange(expert(got_first, w_gate, w_up, w_down, False))
    back_second = exchange(expert(got_second, w_gate, w_up, w_down, True))
    first, second = combine_first(back_first, main_weight, resid[0], projected)
    return combine_second(
        back_second, main_weight, ninth_weight, in_hbm(first), in_hbm(second)
    )[None]


def solution(mesh):
    in_specs = (
        P("exp", "seq", None),
        P("exp", "seq", None),
        P("exp", "seq", None),
        P("exp", "seq", None),
        P("exp", None, "seq", None),
        P("exp", None, "seq", None),
        P("exp"),
        P("seq", None),
        P(),
        P(),
        P("exp", "seq", None),
        P(("seq", "exp"), None, None),
        P(("seq", "exp"), None, None),
        P(("seq", "exp"), None, None),
    )
    out_specs = P("exp", "seq", None)
    return jax.shard_map(
        per_device, mesh=mesh, in_specs=in_specs, out_specs=out_specs, check_vma=False
    )
```

```python
import functools

import jax
import jax.numpy as jnp
import numpy as np
from jax import lax
from jax.experimental import pallas as pl
from jax.experimental.pallas import tpu as pltpu
from jax.sharding import PartitionSpec as P

QUERY_HEAD_HALF = 32
KEY_VALUE_HEADS = 4
HEAD_SIZE = 128
TOP = 8
SLOTS = 8
HALF = SLOTS // 2
GROUP = 256
MIB = 1 << 20


def dot(a, b):
    return jnp.dot(a, b, preferred_element_type=jnp.float32)


def in_hbm(x):
    return pltpu.with_memory_space_constraint(x, pltpu.HBM)


def dot_nt(a, b):
    return lax.dot_general(a, b, (((1,), (1,)), ((), ())), preferred_element_type=jnp.float32)


def pack_kernel(query_ref, key_ref, value_ref, key_cache_ref, value_cache_ref, out_ref, sems):
    parts = out_ref.shape[0]
    cached, tokens = key_cache_ref.shape[2], query_ref.shape[1]
    lanes = query_ref.shape[2] // parts
    ends = [lanes + i * HEAD_SIZE for i in range(4)]
    copies = []
    for s in range(parts):
        head = s * KEY_VALUE_HEADS // parts
        heads = pl.ds(head * HEAD_SIZE, HEAD_SIZE)
        moves = [
            (query_ref.at[0, :, pl.ds(s * lanes, lanes)], out_ref.at[s, :, pl.ds(0, lanes)]),
            (key_ref.at[0, :, heads], out_ref.at[s, :, pl.ds(ends[0], HEAD_SIZE)]),
            (value_ref.at[0, :, heads], out_ref.at[s, :, pl.ds(ends[1], HEAD_SIZE)]),
            (
                key_cache_ref.at[0, head],
                out_ref.at[s, pl.ds(0, cached), pl.ds(ends[2], HEAD_SIZE)],
            ),
            (
                value_cache_ref.at[0, head],
                out_ref.at[s, pl.ds(cached, tokens - cached), pl.ds(ends[2], HEAD_SIZE)],
            ),
        ]
        for i, (source, target) in enumerate(moves):
            copies.append(pltpu.make_async_copy(source, target, sems.at[s, i]))
    for copy in copies:
        copy.start()
    for copy in copies:
        copy.wait()


def pack(queries, keys, values, key_cache, value_cache, seq_count):
    tokens, width = queries.shape[1:]
    cached = key_cache.shape[2]
    assert 2 * cached == tokens
    lanes = width // seq_count
    return pl.pallas_call(
        pack_kernel,
        in_specs=[pl.BlockSpec(memory_space=pltpu.VMEM)] * 5,
        out_specs=pl.BlockSpec(memory_space=pltpu.HBM),
        out_shape=pltpu.HBM((seq_count, tokens, lanes + 3 * HEAD_SIZE), jnp.bfloat16),
        scratch_shapes=[pltpu.SemaphoreType.DMA((seq_count, 5))],
        name="pack",
    )(queries, keys, values, key_cache, value_cache)


def attend_kernel(
    length_ref, packed_ref, out_weight_hbm, out_ref,
    key_ref, value_ref, att_ref, out_weight_ref, sem,
):
    step = pl.program_id(0)
    parts, tokens, _ = packed_ref.shape
    lanes = out_weight_ref.shape[0]
    heads = lanes // HEAD_SIZE
    cached = tokens // 2
    prefix = parts * cached
    rows = out_ref.shape[0]
    per_step = rows // tokens
    rate = HEAD_SIZE ** (-0.5) * float(np.log2(np.e))
    fetch = pltpu.make_async_copy(out_weight_hbm, out_weight_ref, sem)

    @pl.when(step == 0)
    def _():
        fetch.start()
        for t in range(parts):
            old = pl.ds(t * cached, cached)
            new = pl.ds(prefix + t * tokens, tokens)
            key_ref[old, :] = packed_ref[t, :cached, lanes + 2 * HEAD_SIZE :]
            value_ref[old, :] = packed_ref[t, cached:, lanes + 2 * HEAD_SIZE :]
            key_ref[new, :] = packed_ref[t, :, lanes : lanes + HEAD_SIZE]
            value_ref[new, :] = packed_ref[t, :, lanes + HEAD_SIZE : lanes + 2 * HEAD_SIZE]

    in_prefix = lax.broadcasted_iota(jnp.int32, (rows, prefix), 1) < length_ref[0]
    causal = lax.broadcasted_iota(jnp.int32, (rows, rows), 1) <= lax.broadcasted_iota(
        jnp.int32, (rows, rows), 0
    )

    def block(i):
        spans = [(0, prefix)]
        if i:
            spans.append((prefix, i * rows))
        spans.append((prefix + i * rows, rows))
        for h in range(heads):
            query = jnp.concatenate(
                [
                    packed_ref[i * per_step + t, :, h * HEAD_SIZE : (h + 1) * HEAD_SIZE]
                    for t in range(per_step)
                ],
                axis=0,
            )
            scores = [dot_nt(query, key_ref[pl.ds(start, size), :]) for start, size in spans]
            scores[0] = jnp.where(in_prefix, scores[0], -1e30)
            scores[-1] = jnp.where(causal, scores[-1], -1e30)
            top = functools.reduce(
                jnp.maximum, [jnp.max(s, axis=1, keepdims=True) for s in scores]
            )
            total, result = 0.0, 0.0
            for s, (start, size) in zip(scores, spans, strict=True):
                raised = jnp.exp2((s - top) * rate)
                total = total + jnp.sum(raised, axis=1, keepdims=True)
                result = result + dot(
                    raised.astype(jnp.bfloat16), value_ref[pl.ds(start, size), :]
                )
            att_ref[:, h * HEAD_SIZE : (h + 1) * HEAD_SIZE] = (result / total).astype(
                jnp.bfloat16
            )

    for i in range(parts // per_step):
        pl.when(step == i)(functools.partial(block, i))
    pl.when(step == 0)(fetch.wait)
    out_ref[...] = dot(att_ref[...], out_weight_ref[...]).astype(jnp.bfloat16)


def attend(length, packed, out_weight, rows=256):
    parts, tokens, columns = packed.shape
    lanes, width = out_weight.shape
    span = parts * tokens
    total = span + parts * tokens // 2
    return pl.pallas_call(
        attend_kernel,
        grid=(span // rows,),
        in_specs=[
            pl.BlockSpec(memory_space=pltpu.SMEM),
            pl.BlockSpec((parts, tokens, columns), lambda i: (0, 0, 0)),
            pl.BlockSpec(memory_space=pltpu.HBM),
        ],
        out_specs=pl.BlockSpec((rows, width), lambda i: (i, 0)),
        out_shape=jax.ShapeDtypeStruct((span, width), jnp.bfloat16),
        scratch_shapes=[
            pltpu.VMEM((total, HEAD_SIZE), jnp.bfloat16),
            pltpu.VMEM((total, HEAD_SIZE), jnp.bfloat16),
            pltpu.VMEM((rows, lanes), jnp.bfloat16),
            pltpu.VMEM((lanes, width), jnp.bfloat16),
            pltpu.SemaphoreType.DMA,
        ],
        compiler_params=pltpu.CompilerParams(vmem_limit_bytes=48 * MIB),
        name="attend",
    )(length, packed, out_weight)


def named_mask(ids_ref, experts):
    tokens = ids_ref.shape[0]
    lane = lax.broadcasted_iota(jnp.int32, (tokens, experts), 1)
    named = ids_ref[:, 0:1] == lane
    for k in range(1, TOP):
        named = named | (ids_ref[:, k : k + 1] == lane)
    return named


def flags(condition):
    return jnp.where(condition, 1.0, 0.0).astype(jnp.bfloat16)


def spread_flags(experts, axis):
    shape = (experts * SLOTS, experts) if axis == 0 else (experts, experts * SLOTS)
    owner = lax.broadcasted_iota(jnp.int32, shape, axis) // SLOTS
    return flags(owner == lax.broadcasted_iota(jnp.int32, shape, 1 - axis))


def plan_kernel(ids_ref, rank_ref, pick_ref, ninth_ref):
    tokens, experts = rank_ref.shape
    named = named_mask(ids_ref, experts)
    earlier = flags(
        lax.broadcasted_iota(jnp.int32, (tokens, tokens), 0)
        > lax.broadcasted_iota(jnp.int32, (tokens, tokens), 1)
    )
    rank = jnp.where(named, dot(earlier, flags(named)) + 1.0, 0.0)
    rank_ref[...] = rank
    narrow = rank.astype(jnp.bfloat16)
    wide = dot_nt(spread_flags(experts, 0), narrow)
    row = lax.broadcasted_iota(jnp.int32, wide.shape, 0) % SLOTS
    slot = (row % HALF).astype(jnp.float32)
    for chunk in range(2):
        hit = wide == slot + float(1 + HALF * chunk)
        pick_ref[chunk, :, :tokens] = flags(hit & (row < HALF))
        pick_ref[chunk, :, tokens:] = flags(hit & (row >= HALF))
    same = flags(
        lax.broadcasted_iota(jnp.int32, (experts, experts), 0)
        == lax.broadcasted_iota(jnp.int32, (experts, experts), 1)
    )
    ninth_ref[...] = flags(dot_nt(same, narrow) == SLOTS + 1.0)


def plan(ids, experts):
    tokens = ids.shape[0]
    return pl.pallas_call(
        plan_kernel,
        out_shape=[
            pltpu.HBM((tokens, experts), jnp.float32),
            pltpu.HBM((2, experts * SLOTS, 2 * tokens), jnp.bfloat16),
            pltpu.HBM((experts, tokens), jnp.bfloat16),
        ],
        name="plan",
    )(ids)


def route_first_kernel(resid_ref, proj_ref, gain_ref, pick_ref, send_ref, halves_ref):
    step = pl.program_id(0)
    tokens, width = resid_ref.shape
    cols = send_ref.shape[1]
    half = width // 2

    @pl.when(step == 0)
    def _():
        hidden = resid_ref[...].astype(jnp.float32) + proj_ref[...].astype(jnp.float32)
        mean_square = jnp.mean(hidden * hidden, axis=1, keepdims=True)
        normed = (hidden * lax.rsqrt(mean_square + 1e-06) * gain_ref[...]).astype(jnp.bfloat16)
        halves_ref[:tokens, :] = normed[:, :half]
        halves_ref[tokens:, :] = normed[:, half:]

    for j in range(half // cols):

        @pl.when(step == j)
        def _():
            send_ref[...] = dot(
                pick_ref[0], halves_ref[:, j * cols : (j + 1) * cols]
            ).astype(jnp.bfloat16)


def route_first(resid, projected, gain, pick, cols=512):
    tokens, width = resid.shape
    rows, twice = pick.shape[1:]
    half = width // 2
    whole = lambda shape: pl.BlockSpec(shape, lambda j: (0,) * len(shape))
    return pl.pallas_call(
        route_first_kernel,
        grid=(half // cols,),
        in_specs=[
            whole((tokens, width)),
            whole((tokens, width)),
            whole((1, width)),
            whole((1, rows, twice)),
        ],
        out_specs=[pl.BlockSpec((rows, cols), lambda j: (0, j)), whole((twice, half))],
        out_shape=[
            pltpu.HBM((rows, half), jnp.bfloat16),
            pltpu.HBM((twice, half), jnp.bfloat16),
        ],
        compiler_params=pltpu.CompilerParams(vmem_limit_bytes=32 * MIB),
        name="route_first",
    )(resid, projected, gain, pick)


def route_second_kernel(halves_ref, pick_ref, ninth_ref, send_ref, extra_ref):
    step = pl.program_id(0)
    twice, half = halves_ref.shape
    cols = send_ref.shape[1]
    experts, tokens = ninth_ref.shape
    steps = half // cols

    for j in range(steps):

        @pl.when(step == j)
        def _():
            part = halves_ref[:, j * cols : (j + 1) * cols]
            send_ref[...] = dot(pick_ref[0], part).astype(jnp.bfloat16)
            for side in range(2):
                piece = dot(ninth_ref[...], part[side * tokens : (side + 1) * tokens])
                for b in range(cols // 128):
                    extra_ref[b, pl.ds(side * steps + j, experts, stride=SLOTS), :] = piece[
                        :, b * 128 : (b + 1) * 128
                    ]

    @pl.when(step == steps)
    def _():
        for b in range(cols // 128):
            send_ref[:, b * 128 : (b + 1) * 128] = extra_ref[b].astype(jnp.bfloat16)


def route_second(halves, pick, ninth):
    twice, half = halves.shape
    rows = pick.shape[1]
    cols = 2 * half // SLOTS
    whole = lambda shape: pl.BlockSpec(shape, lambda j: (0,) * len(shape))
    return pl.pallas_call(
        route_second_kernel,
        grid=(half // cols + 1,),
        in_specs=[
            whole((twice, half)),
            pl.BlockSpec((1, rows, twice), lambda j: (1, 0, 0)),
            whole(ninth.shape),
        ],
        out_specs=pl.BlockSpec((rows, cols), lambda j: (0, j)),
        out_shape=pltpu.HBM((rows, half + cols), jnp.bfloat16),
        scratch_shapes=[pltpu.VMEM((cols // 128, rows, 128), jnp.float32)],
        compiler_params=pltpu.CompilerParams(vmem_limit_bytes=32 * MIB),
        name="route_second",
    )(halves, pick, ninth)


def weights_kernel(halves_ref, router_ref, rank_ref, main_ref, ninth_ref):
    tokens, experts = rank_ref.shape
    half = halves_ref.shape[1]
    rank = rank_ref[...]
    named = rank > 0.0
    logits = dot(halves_ref[:tokens, :], router_ref[:half, :]) + dot(
        halves_ref[tokens:, :], router_ref[half:, :]
    )
    top = jnp.max(jnp.where(named, logits, -jnp.inf), axis=1, keepdims=True)
    raised = jnp.where(named, jnp.exp(jnp.where(named, logits, top) - top), 0.0)
    weight = raised / jnp.sum(raised, axis=1, keepdims=True)
    high = weight.astype(jnp.bfloat16)
    low = (weight - high.astype(jnp.float32)).astype(jnp.bfloat16)
    spread = spread_flags(experts, 1)
    wide_rank = dot(rank.astype(jnp.bfloat16), spread)
    row = lax.broadcasted_iota(jnp.int32, wide_rank.shape, 1) % SLOTS
    slot = (row % HALF).astype(jnp.float32)
    for term, part in enumerate((high, low)):
        place = pl.ds(term * tokens, tokens)
        wide = dot(part, spread)
        for chunk in range(2):
            kept = jnp.where(wide_rank == slot + float(1 + HALF * chunk), wide, 0.0)
            main_ref[chunk, 0, place, :] = jnp.where(row < HALF, kept, 0.0).astype(jnp.bfloat16)
            main_ref[chunk, 1, place, :] = jnp.where(row >= HALF, kept, 0.0).astype(jnp.bfloat16)
        ninth_ref[place, :] = jnp.where(
            rank == SLOTS + 1.0, part.astype(jnp.float32), 0.0
        ).astype(jnp.bfloat16)


def weights(halves, router, rank):
    tokens, experts = rank.shape
    return pl.pallas_call(
        weights_kernel,
        out_shape=[
            pltpu.HBM((2, 2, 2 * tokens, experts * SLOTS), jnp.bfloat16),
            pltpu.HBM((2 * tokens, experts), jnp.bfloat16),
        ],
        compiler_params=pltpu.CompilerParams(vmem_limit_bytes=32 * MIB),
        name="weights",
    )(halves, router, rank)


def sort_rows():
    to = lax.broadcasted_iota(jnp.int32, (GROUP, GROUP), 0)
    source = lax.broadcasted_iota(jnp.int32, (GROUP, GROUP), 1)
    count = GROUP // 2
    side, index = to // count, to % count
    return flags(source == index // HALF * SLOTS + side * HALF + index % HALF)


def sort_pieces():
    to = lax.broadcasted_iota(jnp.int32, (GROUP, GROUP), 0)
    source = lax.broadcasted_iota(jnp.int32, (GROUP, GROUP), 1)
    count = GROUP // SLOTS
    return flags(source == to % count * SLOTS + to // count)


def dot_tn(a, b):
    return lax.dot_general(a, b, (((0,), (0,)), ((), ())), preferred_element_type=jnp.float32)


def expert_kernel(*refs, deep, ninth):
    rows_ref, refs = refs[0], refs[1:]
    gate_ref, up_ref, first_ref, second_ref, out_ref = refs[:5]
    token_ref, gate_acc, up_acc, act_ref, piece_ref = refs[5:]
    step = pl.program_id(0)
    groups = out_ref.shape[0] // GROUP
    count = GROUP // 2
    few = GROUP // SLOTS
    main = groups * count
    cols = out_ref.shape[1]
    half = rows_ref.shape[1] - (cols if ninth else 0)
    deep_cols = gate_ref.shape[1]
    steps = half // cols

    @pl.when(step < groups)
    def _():
        g = jnp.minimum(step, groups - 1)
        place = pl.ds(pl.multiple_of(g * count, count), count)
        lined = dot(sort_rows(), rows_ref[:, :half]).astype(jnp.bfloat16)
        for k in range(deep):
            side, lane = divmod(k * deep_cols, half)
            token_ref[k, place, :] = lined[
                side * count : (side + 1) * count, lane : lane + deep_cols
            ]
        if ninth:
            place = pl.ds(pl.multiple_of(main + g * few, few), few)
            pieces = dot(sort_pieces(), rows_ref[:, half:]).astype(jnp.bfloat16)
            for j in range(SLOTS):
                k, lane = divmod(j * cols, deep_cols)
                token_ref[k, place, lane : lane + cols] = pieces[j * few : (j + 1) * few]

    start = groups

    @pl.when(step == start)
    def _():
        gate_acc[...] = dot(token_ref[0], gate_ref[0])
        up_acc[...] = dot(token_ref[0], up_ref[0])

    @pl.when((step > start) & (step < start + deep))
    def _():
        rows = token_ref[jnp.clip(step - start, 0, deep - 1)]
        gate_acc[...] += dot(rows, gate_ref[0])
        up_acc[...] += dot(rows, up_ref[0])

    @pl.when(step == start + deep - 1)
    def _():
        gate_val = gate_acc[...]
        act_ref[...] = (gate_val / (1.0 + jnp.exp(-gate_val)) * up_acc[...]).astype(jnp.bfloat16)

    start = groups + deep

    @pl.when((step >= start) & (step < start + steps))
    def _():
        act = act_ref[...]
        sides = [dot(act, ref[0]).astype(jnp.bfloat16) for ref in (first_ref, second_ref)]
        order = sort_rows()
        for g in range(groups):
            part = jnp.concatenate([side[g * count : (g + 1) * count] for side in sides], axis=0)
            out_ref[g * GROUP : (g + 1) * GROUP, :] = dot_tn(order, part).astype(jnp.bfloat16)
        if ninth:
            j = jnp.clip(step - start, 0, steps - 1)
            for which, side in enumerate(sides):
                piece_ref[j + which * steps] = side[main:]

    if ninth:

        @pl.when(step == start + steps)
        def _():
            order = sort_pieces()
            for g in range(groups):
                part = jnp.concatenate(
                    [piece_ref[j, g * few : (g + 1) * few, :] for j in range(SLOTS)], axis=0
                )
                out_ref[g * GROUP : (g + 1) * GROUP, :] = dot_tn(order, part).astype(jnp.bfloat16)


def expert(rows, w_gate, w_up, w_down, ninth, deep=4):
    tall, columns = rows.shape
    _, width, hidden = w_gate.shape
    half, cols = width // 2, width // SLOTS
    assert columns == half + (cols if ninth else 0) and tall % GROUP == 0
    groups, steps = tall // GROUP, half // cols
    main = tall // 2 + (tall // SLOTS if ninth else 0)
    at = groups + deep
    inner = lambda s, begin, count: jnp.clip(s - begin, 0, count - 1)
    weight = pl.BlockSpec((1, width // deep, hidden), lambda s: (0, inner(s, groups, deep), 0))
    return pl.pallas_call(
        functools.partial(expert_kernel, deep=deep, ninth=ninth),
        grid=(at + steps + ninth,),
        in_specs=[
            pl.BlockSpec((GROUP, columns), lambda s: (inner(s, 0, groups), 0)),
            weight,
            weight,
            pl.BlockSpec((1, hidden, cols), lambda s: (0, 0, inner(s, at, steps))),
            pl.BlockSpec((1, hidden, cols), lambda s: (0, 0, steps + inner(s, at, steps))),
        ],
        out_specs=pl.BlockSpec((tall, cols), lambda s: (0, inner(s, at, steps + ninth))),
        out_shape=pltpu.HBM(rows.shape, jnp.bfloat16),
        scratch_shapes=[
            pltpu.VMEM((deep, main, width // deep), jnp.bfloat16),
            pltpu.VMEM((main, hidden), jnp.float32),
            pltpu.VMEM((main, hidden), jnp.float32),
            pltpu.VMEM((main, hidden), jnp.bfloat16),
            pltpu.VMEM((SLOTS, tall // SLOTS, cols), jnp.bfloat16),
        ],
        compiler_params=pltpu.CompilerParams(vmem_limit_bytes=40 * MIB),
        name="expert_second" if ninth else "expert_first",
    )(rows, w_gate, w_up, w_down, w_down)


def combine_first_kernel(rows_ref, weight_ref, *refs):
    resids, projs, outs = refs[:2], refs[2:4], refs[4:]
    tokens = outs[0].shape[0]
    for side in range(2):
        both = dot(weight_ref[0, side], rows_ref[...])
        hidden = resids[side][...].astype(jnp.float32) + projs[side][...].astype(jnp.float32)
        outs[side][...] = hidden + (both[:tokens] + both[tokens:])


def combine_first(rows, main_weight, resid, projected):
    tokens, width = resid.shape
    tall, half = rows.shape
    cols = width // SLOTS
    steps = half // cols
    first = pl.BlockSpec((tokens, cols), lambda j: (0, j))
    second = pl.BlockSpec((tokens, cols), lambda j: (0, steps + j))
    shape = pltpu.HBM((tokens, half), jnp.float32)
    return pl.pallas_call(
        combine_first_kernel,
        grid=(steps,),
        in_specs=[
            pl.BlockSpec((tall, cols), lambda j: (0, j)),
            pl.BlockSpec((1,) + main_weight.shape[1:], lambda j: (0, 0, 0, 0)),
            first,
            second,
            first,
            second,
        ],
        out_specs=[first, first],
        out_shape=[shape, shape],
        compiler_params=pltpu.CompilerParams(vmem_limit_bytes=32 * MIB),
        name="combine_first",
    )(rows, main_weight, resid, resid, projected, projected)


def combine_second_kernel(
    rows_ref, extra_ref, weight_ref, ninth_ref, first_ref, second_ref, out_ref, piece_ref
):
    step = pl.program_id(0)
    tall, cols = rows_ref.shape
    tokens = out_ref.shape[0]
    groups, few = tall // GROUP, GROUP // SLOTS
    steps = SLOTS // 2

    @pl.when(step == 0)
    def _():
        order = sort_pieces()
        for g in range(groups):
            pieces = dot(order, extra_ref[g * GROUP : (g + 1) * GROUP, :]).astype(jnp.bfloat16)
            for j in range(SLOTS):
                piece_ref[j, g * few : (g + 1) * few, :] = pieces[j * few : (j + 1) * few]

    for j in range(steps):

        @pl.when(step == j)
        def _():
            for side, ref in enumerate((first_ref, second_ref)):
                piece = side * steps + j
                both = dot(weight_ref[0, side], rows_ref[...]) + dot(
                    ninth_ref[...], piece_ref[piece]
                )
                out_ref[:, piece * cols : (piece + 1) * cols] = (
                    ref[...] + (both[:tokens] + both[tokens:])
                ).astype(jnp.bfloat16)


def combine_second(rows, main_weight, ninth_weight, first, second):
    tokens, half = first.shape
    tall = rows.shape[0]
    cols = 2 * half // SLOTS
    steps = half // cols
    part = pl.BlockSpec((tokens, cols), lambda j: (0, j))
    return pl.pallas_call(
        combine_second_kernel,
        grid=(steps,),
        in_specs=[
            pl.BlockSpec((tall, cols), lambda j: (0, j)),
            pl.BlockSpec((tall, cols), lambda j: (0, steps)),
            pl.BlockSpec((1,) + main_weight.shape[1:], lambda j: (1, 0, 0, 0)),
            pl.BlockSpec(ninth_weight.shape, lambda j: (0, 0)),
            part,
            part,
        ],
        out_specs=pl.BlockSpec((tokens, 2 * half), lambda j: (0, 0)),
        out_shape=jax.ShapeDtypeStruct((tokens, 2 * half), jnp.bfloat16),
        scratch_shapes=[pltpu.VMEM((SLOTS, tall // SLOTS, cols), jnp.bfloat16)],
        compiler_params=pltpu.CompilerParams(vmem_limit_bytes=32 * MIB),
        name="combine_second",
    )(rows, rows, main_weight, ninth_weight, first, second)


def per_device(
    resid,
    queries,
    span_rotated_keys,
    span_value_rows,
    key_cache,
    prefix_value_cache,
    prefix_len,
    out_weight,
    norm_gain,
    router_weight,
    expert_ids,
    w_gate,
    w_up,
    w_down,
):
    seq_count = lax.axis_size("seq")
    width = resid.shape[2]
    experts = router_weight.shape[1]
    packed = pack(
        queries, span_rotated_keys, span_value_rows, key_cache, prefix_value_cache, seq_count
    )
    packed = lax.all_to_all(packed, "seq", split_axis=0, concat_axis=0, tiled=True)
    projected = lax.psum_scatter(
        attend(prefix_len, packed, in_hbm(out_weight)), "seq", scatter_dimension=0, tiled=True
    )
    projected = in_hbm(projected)
    rank, pick, ninth = [in_hbm(x) for x in plan(expert_ids[0], experts)]
    send_first, halves = route_first(resid[0], projected, norm_gain.reshape(1, width), pick)

    def exchange(rows):
        blocks = rows.reshape(experts, SLOTS, rows.shape[1])
        return in_hbm(
            lax.all_to_all(
                blocks, ("seq", "exp"), split_axis=0, concat_axis=0, tiled=True
            ).reshape(rows.shape)
        )

    halves = in_hbm(halves)
    w_gate, w_up, w_down = in_hbm(w_gate), in_hbm(w_up), in_hbm(w_down)
    got_first = exchange(send_first)
    got_second = exchange(route_second(halves, pick, ninth))
    main_weight, ninth_weight = [in_hbm(x) for x in weights(halves, router_weight, rank)]
    back_first = exchange(expert(got_first, w_gate, w_up, w_down, False))
    back_second = exchange(expert(got_second, w_gate, w_up, w_down, True))
    first, second = combine_first(back_first, main_weight, resid[0], projected)
    return combine_second(
        back_second, main_weight, ninth_weight, in_hbm(first), in_hbm(second)
    )[None]


def solution(mesh):
    in_specs = (
        P("exp", "seq", None),
        P("exp", "seq", None),
        P("exp", "seq", None),
        P("exp", "seq", None),
        P("exp", None, "seq", None),
        P("exp", None, "seq", None),
        P("exp"),
        P("seq", None),
        P(),
        P(),
        P("exp", "seq", None),
        P(("seq", "exp"), None, None),
        P(("seq", "exp"), None, None),
        P(("seq", "exp"), None, None),
    )
    out_specs = P("exp", "seq", None)
    return jax.shard_map(
        per_device, mesh=mesh, in_specs=in_specs, out_specs=out_specs, check_vma=False
    )
```

```python
import functools

import jax
import jax.numpy as jnp
import numpy as np
from jax import lax
from jax.experimental import pallas as pl
from jax.experimental.pallas import tpu as pltpu
from jax.sharding import PartitionSpec as P

QUERY_HEAD_HALF = 32
KEY_VALUE_HEADS = 4
HEAD_SIZE = 128
TOP = 8
SLOTS = 8
HALF = SLOTS // 2
GROUP = 256
MIB = 1 << 20


def dot(a, b):
    return jnp.dot(a, b, preferred_element_type=jnp.float32)


def in_hbm(x):
    return pltpu.with_memory_space_constraint(x, pltpu.HBM)


def dot_nt(a, b):
    return lax.dot_general(a, b, (((1,), (1,)), ((), ())), preferred_element_type=jnp.float32)


def pack_kernel(query_ref, key_ref, value_ref, key_cache_ref, value_cache_ref, out_ref, sems):
    parts = out_ref.shape[0]
    cached, tokens = key_cache_ref.shape[2], query_ref.shape[1]
    lanes = query_ref.shape[2] // parts
    ends = [lanes + i * HEAD_SIZE for i in range(4)]
    copies = []
    for s in range(parts):
        head = s * KEY_VALUE_HEADS // parts
        heads = pl.ds(head * HEAD_SIZE, HEAD_SIZE)
        moves = [
            (query_ref.at[0, :, pl.ds(s * lanes, lanes)], out_ref.at[s, :, pl.ds(0, lanes)]),
            (key_ref.at[0, :, heads], out_ref.at[s, :, pl.ds(ends[0], HEAD_SIZE)]),
            (value_ref.at[0, :, heads], out_ref.at[s, :, pl.ds(ends[1], HEAD_SIZE)]),
            (
                key_cache_ref.at[0, head],
                out_ref.at[s, pl.ds(0, cached), pl.ds(ends[2], HEAD_SIZE)],
            ),
            (
                value_cache_ref.at[0, head],
                out_ref.at[s, pl.ds(cached, tokens - cached), pl.ds(ends[2], HEAD_SIZE)],
            ),
        ]
        for i, (source, target) in enumerate(moves):
            copies.append(pltpu.make_async_copy(source, target, sems.at[s, i]))
    for copy in copies:
        copy.start()
    for copy in copies:
        copy.wait()


def pack(queries, keys, values, key_cache, value_cache, seq_count):
    tokens, width = queries.shape[1:]
    cached = key_cache.shape[2]
    assert 2 * cached == tokens
    lanes = width // seq_count
    return pl.pallas_call(
        pack_kernel,
        in_specs=[pl.BlockSpec(memory_space=pltpu.VMEM)] * 5,
        out_specs=pl.BlockSpec(memory_space=pltpu.HBM),
        out_shape=pltpu.HBM((seq_count, tokens, lanes + 3 * HEAD_SIZE), jnp.bfloat16),
        scratch_shapes=[pltpu.SemaphoreType.DMA((seq_count, 5))],
        name="pack",
    )(queries, keys, values, key_cache, value_cache)


def attend_kernel(
    length_ref, packed_ref, out_weight_hbm, out_ref,
    key_ref, value_ref, att_ref, out_weight_ref, sem,
):
    step = pl.program_id(0)
    parts, tokens, _ = packed_ref.shape
    lanes = out_weight_ref.shape[0]
    heads = lanes // HEAD_SIZE
    cached = tokens // 2
    prefix = parts * cached
    rows = out_ref.shape[0]
    per_step = rows // tokens
    rate = HEAD_SIZE ** (-0.5) * float(np.log2(np.e))
    fetch = pltpu.make_async_copy(out_weight_hbm, out_weight_ref, sem)

    @pl.when(step == 0)
    def _():
        fetch.start()
        for t in range(parts):
            old = pl.ds(t * cached, cached)
            new = pl.ds(prefix + t * tokens, tokens)
            key_ref[old, :] = packed_ref[t, :cached, lanes + 2 * HEAD_SIZE :]
            value_ref[old, :] = packed_ref[t, cached:, lanes + 2 * HEAD_SIZE :]
            key_ref[new, :] = packed_ref[t, :, lanes : lanes + HEAD_SIZE]
            value_ref[new, :] = packed_ref[t, :, lanes + HEAD_SIZE : lanes + 2 * HEAD_SIZE]

    in_prefix = lax.broadcasted_iota(jnp.int32, (rows, prefix), 1) < length_ref[0]
    causal = lax.broadcasted_iota(jnp.int32, (rows, rows), 1) <= lax.broadcasted_iota(
        jnp.int32, (rows, rows), 0
    )

    def block(i):
        spans = [(0, prefix)]
        if i:
            spans.append((prefix, i * rows))
        spans.append((prefix + i * rows, rows))
        for h in range(heads):
            query = jnp.concatenate(
                [
                    packed_ref[i * per_step + t, :, h * HEAD_SIZE : (h + 1) * HEAD_SIZE]
                    for t in range(per_step)
                ],
                axis=0,
            )
            scores = [dot_nt(query, key_ref[pl.ds(start, size), :]) for start, size in spans]
            scores[0] = jnp.where(in_prefix, scores[0], -1e30)
            scores[-1] = jnp.where(causal, scores[-1], -1e30)
            top = functools.reduce(
                jnp.maximum, [jnp.max(s, axis=1, keepdims=True) for s in scores]
            )
            total, result = 0.0, 0.0
            for s, (start, size) in zip(scores, spans, strict=True):
                raised = jnp.exp2((s - top) * rate)
                total = total + jnp.sum(raised, axis=1, keepdims=True)
                result = result + dot(
                    raised.astype(jnp.bfloat16), value_ref[pl.ds(start, size), :]
                )
            att_ref[:, h * HEAD_SIZE : (h + 1) * HEAD_SIZE] = (result / total).astype(
                jnp.bfloat16
            )

    for i in range(parts // per_step):
        pl.when(step == i)(functools.partial(block, i))
    pl.when(step == 0)(fetch.wait)
    out_ref[...] = dot(att_ref[...], out_weight_ref[...]).astype(jnp.bfloat16)


def attend(length, packed, out_weight, rows=512):
    parts, tokens, columns = packed.shape
    lanes, width = out_weight.shape
    span = parts * tokens
    total = span + parts * tokens // 2
    return pl.pallas_call(
        attend_kernel,
        grid=(span // rows,),
        in_specs=[
            pl.BlockSpec(memory_space=pltpu.SMEM),
            pl.BlockSpec(memory_space=pltpu.VMEM),
            pl.BlockSpec(memory_space=pltpu.HBM),
        ],
        out_specs=pl.BlockSpec((rows, width), lambda i: (i, 0)),
        out_shape=jax.ShapeDtypeStruct((span, width), jnp.bfloat16),
        scratch_shapes=[
            pltpu.VMEM((total, HEAD_SIZE), jnp.bfloat16),
            pltpu.VMEM((total, HEAD_SIZE), jnp.bfloat16),
            pltpu.VMEM((rows, lanes), jnp.bfloat16),
            pltpu.VMEM((lanes, width), jnp.bfloat16),
            pltpu.SemaphoreType.DMA,
        ],
        compiler_params=pltpu.CompilerParams(vmem_limit_bytes=48 * MIB),
        name="attend",
    )(length, packed, out_weight)


def named_mask(ids_ref, experts):
    tokens = ids_ref.shape[0]
    lane = lax.broadcasted_iota(jnp.int32, (tokens, experts), 1)
    named = ids_ref[:, 0:1] == lane
    for k in range(1, TOP):
        named = named | (ids_ref[:, k : k + 1] == lane)
    return named


def flags(condition):
    return jnp.where(condition, 1.0, 0.0).astype(jnp.bfloat16)


def spread_flags(experts, axis):
    shape = (experts * SLOTS, experts) if axis == 0 else (experts, experts * SLOTS)
    owner = lax.broadcasted_iota(jnp.int32, shape, axis) // SLOTS
    return flags(owner == lax.broadcasted_iota(jnp.int32, shape, 1 - axis))


def plan_kernel(ids_ref, rank_ref, pick_ref, ninth_ref):
    tokens, experts = rank_ref.shape
    named = named_mask(ids_ref, experts)
    earlier = flags(
        lax.broadcasted_iota(jnp.int32, (tokens, tokens), 0)
        > lax.broadcasted_iota(jnp.int32, (tokens, tokens), 1)
    )
    rank = jnp.where(named, dot(earlier, flags(named)) + 1.0, 0.0)
    rank_ref[...] = rank
    narrow = rank.astype(jnp.bfloat16)
    wide = dot_nt(spread_flags(experts, 0), narrow)
    row = lax.broadcasted_iota(jnp.int32, wide.shape, 0) % SLOTS
    slot = (row % HALF).astype(jnp.float32)
    for chunk in range(2):
        hit = wide == slot + float(1 + HALF * chunk)
        pick_ref[chunk, :, :tokens] = flags(hit & (row < HALF))
        pick_ref[chunk, :, tokens:] = flags(hit & (row >= HALF))
    same = flags(
        lax.broadcasted_iota(jnp.int32, (experts, experts), 0)
        == lax.broadcasted_iota(jnp.int32, (experts, experts), 1)
    )
    ninth_ref[...] = flags(dot_nt(same, narrow) == SLOTS + 1.0)


def plan(ids, experts):
    tokens = ids.shape[0]
    return pl.pallas_call(
        plan_kernel,
        out_shape=[
            pltpu.HBM((tokens, experts), jnp.float32),
            pltpu.HBM((2, experts * SLOTS, 2 * tokens), jnp.bfloat16),
            pltpu.HBM((experts, tokens), jnp.bfloat16),
        ],
        name="plan",
    )(ids)


def route_first_kernel(resid_ref, proj_ref, gain_ref, pick_ref, send_ref, halves_ref):
    step = pl.program_id(0)
    tokens, width = resid_ref.shape
    cols = send_ref.shape[1]
    half = width // 2

    @pl.when(step == 0)
    def _():
        hidden = resid_ref[...].astype(jnp.float32) + proj_ref[...].astype(jnp.float32)
        mean_square = jnp.mean(hidden * hidden, axis=1, keepdims=True)
        normed = (hidden * lax.rsqrt(mean_square + 1e-06) * gain_ref[...]).astype(jnp.bfloat16)
        halves_ref[:tokens, :] = normed[:, :half]
        halves_ref[tokens:, :] = normed[:, half:]

    for j in range(half // cols):

        @pl.when(step == j)
        def _():
            send_ref[...] = dot(
                pick_ref[0], halves_ref[:, j * cols : (j + 1) * cols]
            ).astype(jnp.bfloat16)


def route_first(resid, projected, gain, pick, cols=1024):
    tokens, width = resid.shape
    rows, twice = pick.shape[1:]
    half = width // 2
    whole = lambda shape: pl.BlockSpec(shape, lambda j: (0,) * len(shape))
    return pl.pallas_call(
        route_first_kernel,
        grid=(half // cols,),
        in_specs=[
            whole((tokens, width)),
            whole((tokens, width)),
            whole((1, width)),
            whole((1, rows, twice)),
        ],
        out_specs=[pl.BlockSpec((rows, cols), lambda j: (0, j)), whole((twice, half))],
        out_shape=[
            pltpu.HBM((rows, half), jnp.bfloat16),
            pltpu.HBM((twice, half), jnp.bfloat16),
        ],
        compiler_params=pltpu.CompilerParams(vmem_limit_bytes=32 * MIB),
        name="route_first",
    )(resid, projected, gain, pick)


def route_second_kernel(halves_ref, pick_ref, ninth_ref, send_ref, extra_ref):
    step = pl.program_id(0)
    twice, half = halves_ref.shape
    cols = send_ref.shape[1]
    experts, tokens = ninth_ref.shape
    steps = half // cols

    for j in range(steps):

        @pl.when(step == j)
        def _():
            part = halves_ref[:, j * cols : (j + 1) * cols]
            send_ref[...] = dot(pick_ref[0], part).astype(jnp.bfloat16)
            for side in range(2):
                piece = dot(ninth_ref[...], part[side * tokens : (side + 1) * tokens])
                for b in range(cols // 128):
                    extra_ref[b, pl.ds(side * steps + j, experts, stride=SLOTS), :] = piece[
                        :, b * 128 : (b + 1) * 128
                    ]

    @pl.when(step == steps)
    def _():
        for b in range(cols // 128):
            send_ref[:, b * 128 : (b + 1) * 128] = extra_ref[b].astype(jnp.bfloat16)


def route_second(halves, pick, ninth):
    twice, half = halves.shape
    rows = pick.shape[1]
    cols = 2 * half // SLOTS
    whole = lambda shape: pl.BlockSpec(shape, lambda j: (0,) * len(shape))
    return pl.pallas_call(
        route_second_kernel,
        grid=(half // cols + 1,),
        in_specs=[
            whole((twice, half)),
            pl.BlockSpec((1, rows, twice), lambda j: (1, 0, 0)),
            whole(ninth.shape),
        ],
        out_specs=pl.BlockSpec((rows, cols), lambda j: (0, j)),
        out_shape=pltpu.HBM((rows, half + cols), jnp.bfloat16),
        scratch_shapes=[pltpu.VMEM((cols // 128, rows, 128), jnp.float32)],
        compiler_params=pltpu.CompilerParams(vmem_limit_bytes=32 * MIB),
        name="route_second",
    )(halves, pick, ninth)


def weights_kernel(halves_ref, router_ref, rank_ref, main_ref, ninth_ref):
    tokens, experts = rank_ref.shape
    half = halves_ref.shape[1]
    rank = rank_ref[...]
    named = rank > 0.0
    logits = dot(halves_ref[:tokens, :], router_ref[:half, :]) + dot(
        halves_ref[tokens:, :], router_ref[half:, :]
    )
    top = jnp.max(jnp.where(named, logits, -jnp.inf), axis=1, keepdims=True)
    raised = jnp.where(named, jnp.exp(jnp.where(named, logits, top) - top), 0.0)
    weight = raised / jnp.sum(raised, axis=1, keepdims=True)
    high = weight.astype(jnp.bfloat16)
    low = (weight - high.astype(jnp.float32)).astype(jnp.bfloat16)
    spread = spread_flags(experts, 1)
    wide_rank = dot(rank.astype(jnp.bfloat16), spread)
    row = lax.broadcasted_iota(jnp.int32, wide_rank.shape, 1) % SLOTS
    slot = (row % HALF).astype(jnp.float32)
    for term, part in enumerate((high, low)):
        place = pl.ds(term * tokens, tokens)
        wide = dot(part, spread)
        for chunk in range(2):
            kept = jnp.where(wide_rank == slot + float(1 + HALF * chunk), wide, 0.0)
            main_ref[chunk, 0, place, :] = jnp.where(row < HALF, kept, 0.0).astype(jnp.bfloat16)
            main_ref[chunk, 1, place, :] = jnp.where(row >= HALF, kept, 0.0).astype(jnp.bfloat16)
        ninth_ref[place, :] = jnp.where(
            rank == SLOTS + 1.0, part.astype(jnp.float32), 0.0
        ).astype(jnp.bfloat16)


def weights(halves, router, rank):
    tokens, experts = rank.shape
    return pl.pallas_call(
        weights_kernel,
        out_shape=[
            pltpu.HBM((2, 2, 2 * tokens, experts * SLOTS), jnp.bfloat16),
            pltpu.HBM((2 * tokens, experts), jnp.bfloat16),
        ],
        compiler_params=pltpu.CompilerParams(vmem_limit_bytes=32 * MIB),
        name="weights",
    )(halves, router, rank)


def sort_rows():
    to = lax.broadcasted_iota(jnp.int32, (GROUP, GROUP), 0)
    source = lax.broadcasted_iota(jnp.int32, (GROUP, GROUP), 1)
    count = GROUP // 2
    side, index = to // count, to % count
    return flags(source == index // HALF * SLOTS + side * HALF + index % HALF)


def sort_pieces():
    to = lax.broadcasted_iota(jnp.int32, (GROUP, GROUP), 0)
    source = lax.broadcasted_iota(jnp.int32, (GROUP, GROUP), 1)
    count = GROUP // SLOTS
    return flags(source == to % count * SLOTS + to // count)


def dot_tn(a, b):
    return lax.dot_general(a, b, (((0,), (0,)), ((), ())), preferred_element_type=jnp.float32)


def expert_kernel(*refs, deep, ninth):
    rows_ref, refs = refs[0], refs[1:]
    gate_ref, up_ref, first_ref, second_ref, out_ref = refs[:5]
    token_ref, gate_acc, up_acc, act_ref, piece_ref = refs[5:]
    step = pl.program_id(0)
    groups = out_ref.shape[0] // GROUP
    count = GROUP // 2
    few = GROUP // SLOTS
    main = groups * count
    cols = out_ref.shape[1]
    half = rows_ref.shape[1] - (cols if ninth else 0)
    deep_cols = gate_ref.shape[1]
    steps = half // cols

    @pl.when(step < groups)
    def _():
        g = jnp.minimum(step, groups - 1)
        place = pl.ds(pl.multiple_of(g * count, count), count)
        lined = dot(sort_rows(), rows_ref[:, :half]).astype(jnp.bfloat16)
        for k in range(deep):
            side, lane = divmod(k * deep_cols, half)
            token_ref[k, place, :] = lined[
                side * count : (side + 1) * count, lane : lane + deep_cols
            ]
        if ninth:
            place = pl.ds(pl.multiple_of(main + g * few, few), few)
            pieces = dot(sort_pieces(), rows_ref[:, half:]).astype(jnp.bfloat16)
            for j in range(SLOTS):
                k, lane = divmod(j * cols, deep_cols)
                token_ref[k, place, lane : lane + cols] = pieces[j * few : (j + 1) * few]

    start = groups

    @pl.when(step == start)
    def _():
        gate_acc[...] = dot(token_ref[0], gate_ref[0])
        up_acc[...] = dot(token_ref[0], up_ref[0])

    @pl.when((step > start) & (step < start + deep))
    def _():
        rows = token_ref[jnp.clip(step - start, 0, deep - 1)]
        gate_acc[...] += dot(rows, gate_ref[0])
        up_acc[...] += dot(rows, up_ref[0])

    @pl.when(step == start + deep - 1)
    def _():
        gate_val = gate_acc[...]
        act_ref[...] = (gate_val / (1.0 + jnp.exp(-gate_val)) * up_acc[...]).astype(jnp.bfloat16)

    start = groups + deep

    @pl.when((step >= start) & (step < start + steps))
    def _():
        act = act_ref[...]
        sides = [dot(act, ref[0]).astype(jnp.bfloat16) for ref in (first_ref, second_ref)]
        order = sort_rows()
        for g in range(groups):
            part = jnp.concatenate([side[g * count : (g + 1) * count] for side in sides], axis=0)
            out_ref[g * GROUP : (g + 1) * GROUP, :] = dot_tn(order, part).astype(jnp.bfloat16)
        if ninth:
            j = jnp.clip(step - start, 0, steps - 1)
            for which, side in enumerate(sides):
                piece_ref[j + which * steps] = side[main:]

    if ninth:

        @pl.when(step == start + steps)
        def _():
            order = sort_pieces()
            for g in range(groups):
                part = jnp.concatenate(
                    [piece_ref[j, g * few : (g + 1) * few, :] for j in range(SLOTS)], axis=0
                )
                out_ref[g * GROUP : (g + 1) * GROUP, :] = dot_tn(order, part).astype(jnp.bfloat16)


def expert(rows, w_gate, w_up, w_down, ninth, deep=4):
    tall, columns = rows.shape
    _, width, hidden = w_gate.shape
    half, cols = width // 2, width // SLOTS
    assert columns == half + (cols if ninth else 0) and tall % GROUP == 0
    groups, steps = tall // GROUP, half // cols
    main = tall // 2 + (tall // SLOTS if ninth else 0)
    at = groups + deep
    inner = lambda s, begin, count: jnp.clip(s - begin, 0, count - 1)
    weight = pl.BlockSpec((1, width // deep, hidden), lambda s: (0, inner(s, groups, deep), 0))
    return pl.pallas_call(
        functools.partial(expert_kernel, deep=deep, ninth=ninth),
        grid=(at + steps + ninth,),
        in_specs=[
            pl.BlockSpec((GROUP, columns), lambda s: (inner(s, 0, groups), 0)),
            weight,
            weight,
            pl.BlockSpec((1, hidden, cols), lambda s: (0, 0, inner(s, at, steps))),
            pl.BlockSpec((1, hidden, cols), lambda s: (0, 0, steps + inner(s, at, steps))),
        ],
        out_specs=pl.BlockSpec((tall, cols), lambda s: (0, inner(s, at, steps + ninth))),
        out_shape=pltpu.HBM(rows.shape, jnp.bfloat16),
        scratch_shapes=[
            pltpu.VMEM((deep, main, width // deep), jnp.bfloat16),
            pltpu.VMEM((main, hidden), jnp.float32),
            pltpu.VMEM((main, hidden), jnp.float32),
            pltpu.VMEM((main, hidden), jnp.bfloat16),
            pltpu.VMEM((SLOTS, tall // SLOTS, cols), jnp.bfloat16),
        ],
        compiler_params=pltpu.CompilerParams(vmem_limit_bytes=40 * MIB),
        name="expert_second" if ninth else "expert_first",
    )(rows, w_gate, w_up, w_down, w_down)


def combine_first_kernel(rows_ref, weight_ref, *refs):
    resids, projs, outs = refs[:2], refs[2:4], refs[4:]
    tokens = outs[0].shape[0]
    for side in range(2):
        both = dot(weight_ref[0, side], rows_ref[...])
        hidden = resids[side][...].astype(jnp.float32) + projs[side][...].astype(jnp.float32)
        outs[side][...] = hidden + (both[:tokens] + both[tokens:])


def combine_first(rows, main_weight, resid, projected):
    tokens, width = resid.shape
    tall, half = rows.shape
    cols = width // SLOTS
    steps = half // cols
    first = pl.BlockSpec((tokens, cols), lambda j: (0, j))
    second = pl.BlockSpec((tokens, cols), lambda j: (0, steps + j))
    shape = pltpu.HBM((tokens, half), jnp.float32)
    return pl.pallas_call(
        combine_first_kernel,
        grid=(steps,),
        in_specs=[
            pl.BlockSpec((tall, cols), lambda j: (0, j)),
            pl.BlockSpec((1,) + main_weight.shape[1:], lambda j: (0, 0, 0, 0)),
            first,
            second,
            first,
            second,
        ],
        out_specs=[first, first],
        out_shape=[shape, shape],
        compiler_params=pltpu.CompilerParams(vmem_limit_bytes=32 * MIB),
        name="combine_first",
    )(rows, main_weight, resid, resid, projected, projected)


def combine_second_kernel(
    rows_ref, extra_ref, weight_ref, ninth_ref, first_ref, second_ref, out_ref, piece_ref
):
    step = pl.program_id(0)
    tall, cols = rows_ref.shape
    small = extra_ref.shape[1]
    tokens, width = out_ref.shape
    groups, few = tall // GROUP, GROUP // SLOTS
    half = width // 2

    @pl.when(step == 0)
    def _():
        order = sort_pieces()
        for g in range(groups):
            pieces = dot(order, extra_ref[g * GROUP : (g + 1) * GROUP, :]).astype(jnp.bfloat16)
            for j in range(SLOTS):
                piece_ref[g * few : (g + 1) * few, j * small : (j + 1) * small] = pieces[
                    j * few : (j + 1) * few
                ]

    for j in range(half // cols):

        @pl.when(step == j)
        def _():
            for side, ref in enumerate((first_ref, second_ref)):
                lanes = slice(side * half + j * cols, side * half + (j + 1) * cols)
                both = dot(weight_ref[0, side], rows_ref[...]) + dot(
                    ninth_ref[...], piece_ref[:, lanes]
                )
                out_ref[:, lanes] = (ref[...] + (both[:tokens] + both[tokens:])).astype(
                    jnp.bfloat16
                )


def combine_second(rows, main_weight, ninth_weight, first, second, cols=1024):
    tokens, half = first.shape
    tall = rows.shape[0]
    small = 2 * half // SLOTS
    part = pl.BlockSpec((tokens, cols), lambda j: (0, j))
    return pl.pallas_call(
        combine_second_kernel,
        grid=(half // cols,),
        in_specs=[
            pl.BlockSpec((tall, cols), lambda j: (0, j)),
            pl.BlockSpec((tall, small), lambda j: (0, half // small)),
            pl.BlockSpec((1,) + main_weight.shape[1:], lambda j: (1, 0, 0, 0)),
            pl.BlockSpec(ninth_weight.shape, lambda j: (0, 0)),
            part,
            part,
        ],
        out_specs=pl.BlockSpec((tokens, 2 * half), lambda j: (0, 0)),
        out_shape=jax.ShapeDtypeStruct((tokens, 2 * half), jnp.bfloat16),
        scratch_shapes=[pltpu.VMEM((tall // SLOTS, 2 * half), jnp.bfloat16)],
        compiler_params=pltpu.CompilerParams(vmem_limit_bytes=32 * MIB),
        name="combine_second",
    )(rows, rows, main_weight, ninth_weight, first, second)


def per_device(
    resid,
    queries,
    span_rotated_keys,
    span_value_rows,
    key_cache,
    prefix_value_cache,
    prefix_len,
    out_weight,
    norm_gain,
    router_weight,
    expert_ids,
    w_gate,
    w_up,
    w_down,
):
    seq_count = lax.axis_size("seq")
    width = resid.shape[2]
    experts = router_weight.shape[1]
    packed = pack(
        queries, span_rotated_keys, span_value_rows, key_cache, prefix_value_cache, seq_count
    )
    packed = lax.all_to_all(packed, "seq", split_axis=0, concat_axis=0, tiled=True)
    projected = lax.psum_scatter(
        attend(prefix_len, packed, in_hbm(out_weight)), "seq", scatter_dimension=0, tiled=True
    )
    projected = in_hbm(projected)
    rank, pick, ninth = [in_hbm(x) for x in plan(expert_ids[0], experts)]
    send_first, halves = route_first(resid[0], projected, norm_gain.reshape(1, width), pick)

    def exchange(rows):
        blocks = rows.reshape(experts, SLOTS, rows.shape[1])
        return in_hbm(
            lax.all_to_all(
                blocks, ("seq", "exp"), split_axis=0, concat_axis=0, tiled=True
            ).reshape(rows.shape)
        )

    halves = in_hbm(halves)
    w_gate, w_up, w_down = in_hbm(w_gate), in_hbm(w_up), in_hbm(w_down)
    got_first = exchange(send_first)
    got_second = exchange(route_second(halves, pick, ninth))
    main_weight, ninth_weight = [in_hbm(x) for x in weights(halves, router_weight, rank)]
    back_first = exchange(expert(got_first, w_gate, w_up, w_down, False))
    back_second = exchange(expert(got_second, w_gate, w_up, w_down, True))
    first, second = combine_first(back_first, main_weight, resid[0], projected)
    return combine_second(
        back_second, main_weight, ninth_weight, in_hbm(first), in_hbm(second)
    )[None]


def solution(mesh):
    in_specs = (
        P("exp", "seq", None),
        P("exp", "seq", None),
        P("exp", "seq", None),
        P("exp", "seq", None),
        P("exp", None, "seq", None),
        P("exp", None, "seq", None),
        P("exp"),
        P("seq", None),
        P(),
        P(),
        P("exp", "seq", None),
        P(("seq", "exp"), None, None),
        P(("seq", "exp"), None, None),
        P(("seq", "exp"), None, None),
    )
    out_specs = P("exp", "seq", None)
    return jax.shard_map(
        per_device, mesh=mesh, in_specs=in_specs, out_specs=out_specs, check_vma=False
    )
```

```python
import functools

import jax
import jax.numpy as jnp
import numpy as np
from jax import lax
from jax.experimental import pallas as pl
from jax.experimental.pallas import tpu as pltpu
from jax.sharding import PartitionSpec as P

QUERY_HEAD_HALF = 32
KEY_VALUE_HEADS = 4
HEAD_SIZE = 128
TOP = 8
SLOTS = 8
HALF = SLOTS // 2
GROUP = 256
MIB = 1 << 20


def dot(a, b):
    return jnp.dot(a, b, preferred_element_type=jnp.float32)


def in_hbm(x):
    return pltpu.with_memory_space_constraint(x, pltpu.HBM)


def dot_nt(a, b):
    return lax.dot_general(a, b, (((1,), (1,)), ((), ())), preferred_element_type=jnp.float32)


def pack_kernel(query_ref, key_ref, value_ref, key_cache_ref, value_cache_ref, out_ref, sems):
    parts = out_ref.shape[0]
    cached, tokens = key_cache_ref.shape[2], query_ref.shape[1]
    lanes = query_ref.shape[2] // parts
    ends = [lanes + i * HEAD_SIZE for i in range(4)]
    copies = []
    for s in range(parts):
        head = s * KEY_VALUE_HEADS // parts
        heads = pl.ds(head * HEAD_SIZE, HEAD_SIZE)
        moves = [
            (query_ref.at[0, :, pl.ds(s * lanes, lanes)], out_ref.at[s, :, pl.ds(0, lanes)]),
            (key_ref.at[0, :, heads], out_ref.at[s, :, pl.ds(ends[0], HEAD_SIZE)]),
            (value_ref.at[0, :, heads], out_ref.at[s, :, pl.ds(ends[1], HEAD_SIZE)]),
            (
                key_cache_ref.at[0, head],
                out_ref.at[s, pl.ds(0, cached), pl.ds(ends[2], HEAD_SIZE)],
            ),
            (
                value_cache_ref.at[0, head],
                out_ref.at[s, pl.ds(cached, tokens - cached), pl.ds(ends[2], HEAD_SIZE)],
            ),
        ]
        for i, (source, target) in enumerate(moves):
            copies.append(pltpu.make_async_copy(source, target, sems.at[s, i]))
    for copy in copies:
        copy.start()
    for copy in copies:
        copy.wait()


def pack(queries, keys, values, key_cache, value_cache, seq_count):
    tokens, width = queries.shape[1:]
    cached = key_cache.shape[2]
    assert 2 * cached == tokens
    lanes = width // seq_count
    return pl.pallas_call(
        pack_kernel,
        in_specs=[pl.BlockSpec(memory_space=pltpu.VMEM)] * 5,
        out_specs=pl.BlockSpec(memory_space=pltpu.HBM),
        out_shape=pltpu.HBM((seq_count, tokens, lanes + 3 * HEAD_SIZE), jnp.bfloat16),
        scratch_shapes=[pltpu.SemaphoreType.DMA((seq_count, 5))],
        name="pack",
    )(queries, keys, values, key_cache, value_cache)


def attend_kernel(
    length_ref, packed_ref, out_weight_hbm, out_ref,
    key_ref, value_ref, att_ref, out_weight_ref, sem,
):
    step = pl.program_id(0)
    parts, tokens, _ = packed_ref.shape
    lanes = out_weight_ref.shape[0]
    heads = lanes // HEAD_SIZE
    cached = tokens // 2
    prefix = parts * cached
    rows = out_ref.shape[0]
    per_step = rows // tokens
    rate = HEAD_SIZE ** (-0.5) * float(np.log2(np.e))
    fetch = pltpu.make_async_copy(out_weight_hbm, out_weight_ref, sem)

    @pl.when(step == 0)
    def _():
        fetch.start()
        for t in range(parts):
            old = pl.ds(t * cached, cached)
            new = pl.ds(prefix + t * tokens, tokens)
            key_ref[old, :] = packed_ref[t, :cached, lanes + 2 * HEAD_SIZE :]
            value_ref[old, :] = packed_ref[t, cached:, lanes + 2 * HEAD_SIZE :]
            key_ref[new, :] = packed_ref[t, :, lanes : lanes + HEAD_SIZE]
            value_ref[new, :] = packed_ref[t, :, lanes + HEAD_SIZE : lanes + 2 * HEAD_SIZE]

    in_prefix = lax.broadcasted_iota(jnp.int32, (rows, prefix), 1) < length_ref[0]
    causal = lax.broadcasted_iota(jnp.int32, (rows, rows), 1) <= lax.broadcasted_iota(
        jnp.int32, (rows, rows), 0
    )

    def block(i):
        spans = [(0, prefix)]
        if i:
            spans.append((prefix, i * rows))
        spans.append((prefix + i * rows, rows))
        for h in range(heads):
            query = jnp.concatenate(
                [
                    packed_ref[i * per_step + t, :, h * HEAD_SIZE : (h + 1) * HEAD_SIZE]
                    for t in range(per_step)
                ],
                axis=0,
            )
            scores = [dot_nt(query, key_ref[pl.ds(start, size), :]) for start, size in spans]
            scores[0] = jnp.where(in_prefix, scores[0], -1e30)
            scores[-1] = jnp.where(causal, scores[-1], -1e30)
            top = functools.reduce(
                jnp.maximum, [jnp.max(s, axis=1, keepdims=True) for s in scores]
            )
            total, result = 0.0, 0.0
            for s, (start, size) in zip(scores, spans, strict=True):
                raised = jnp.exp2((s - top) * rate)
                total = total + jnp.sum(raised, axis=1, keepdims=True)
                result = result + dot(
                    raised.astype(jnp.bfloat16), value_ref[pl.ds(start, size), :]
                )
            att_ref[:, h * HEAD_SIZE : (h + 1) * HEAD_SIZE] = (result / total).astype(
                jnp.bfloat16
            )

    for i in range(parts // per_step):
        pl.when(step == i)(functools.partial(block, i))
    pl.when(step == 0)(fetch.wait)
    out_ref[...] = dot(att_ref[...], out_weight_ref[...]).astype(jnp.bfloat16)


def attend(length, packed, out_weight, rows=512):
    parts, tokens, columns = packed.shape
    lanes, width = out_weight.shape
    span = parts * tokens
    total = span + parts * tokens // 2
    return pl.pallas_call(
        attend_kernel,
        grid=(span // rows,),
        in_specs=[
            pl.BlockSpec(memory_space=pltpu.SMEM),
            pl.BlockSpec(memory_space=pltpu.VMEM),
            pl.BlockSpec(memory_space=pltpu.HBM),
        ],
        out_specs=pl.BlockSpec((rows, width), lambda i: (i, 0)),
        out_shape=jax.ShapeDtypeStruct((span, width), jnp.bfloat16),
        scratch_shapes=[
            pltpu.VMEM((total, HEAD_SIZE), jnp.bfloat16),
            pltpu.VMEM((total, HEAD_SIZE), jnp.bfloat16),
            pltpu.VMEM((rows, lanes), jnp.bfloat16),
            pltpu.VMEM((lanes, width), jnp.bfloat16),
            pltpu.SemaphoreType.DMA,
        ],
        compiler_params=pltpu.CompilerParams(vmem_limit_bytes=48 * MIB),
        name="attend",
    )(length, packed, out_weight)


def named_mask(ids_ref, experts):
    tokens = ids_ref.shape[0]
    lane = lax.broadcasted_iota(jnp.int32, (tokens, experts), 1)
    named = ids_ref[:, 0:1] == lane
    for k in range(1, TOP):
        named = named | (ids_ref[:, k : k + 1] == lane)
    return named


def flags(condition):
    return jnp.where(condition, 1.0, 0.0).astype(jnp.bfloat16)


def spread_flags(experts, axis):
    shape = (experts * SLOTS, experts) if axis == 0 else (experts, experts * SLOTS)
    owner = lax.broadcasted_iota(jnp.int32, shape, axis) // SLOTS
    return flags(owner == lax.broadcasted_iota(jnp.int32, shape, 1 - axis))


def plan_kernel(ids_ref, rank_ref, zero_ref, one_ref, ninth_ref):
    tokens, experts = rank_ref.shape
    named = named_mask(ids_ref, experts)
    earlier = flags(
        lax.broadcasted_iota(jnp.int32, (tokens, tokens), 0)
        > lax.broadcasted_iota(jnp.int32, (tokens, tokens), 1)
    )
    rank = jnp.where(named, dot(earlier, flags(named)) + 1.0, 0.0)
    rank_ref[...] = rank
    narrow = rank.astype(jnp.bfloat16)
    wide = dot_nt(spread_flags(experts, 0), narrow)
    row = lax.broadcasted_iota(jnp.int32, wide.shape, 0) % SLOTS
    slot = (row % HALF).astype(jnp.float32)
    for chunk in range(2):
        hit = wide == slot + float(1 + HALF * chunk)
        pick_ref = (zero_ref, one_ref)[chunk]
        pick_ref[:, :tokens] = flags(hit & (row < HALF))
        pick_ref[:, tokens:] = flags(hit & (row >= HALF))
    same = flags(
        lax.broadcasted_iota(jnp.int32, (experts, experts), 0)
        == lax.broadcasted_iota(jnp.int32, (experts, experts), 1)
    )
    ninth_ref[...] = flags(dot_nt(same, narrow) == SLOTS + 1.0)


def plan(ids, experts):
    tokens = ids.shape[0]
    return pl.pallas_call(
        plan_kernel,
        out_shape=[
            pltpu.HBM((tokens, experts), jnp.float32),
            pltpu.VMEM((experts * SLOTS, 2 * tokens), jnp.bfloat16),
            pltpu.HBM((experts * SLOTS, 2 * tokens), jnp.bfloat16),
            pltpu.HBM((experts, tokens), jnp.bfloat16),
        ],
        name="plan",
    )(ids)


def route_first_kernel(resid_ref, proj_ref, gain_ref, pick_ref, send_ref, halves_ref):
    step = pl.program_id(0)
    tokens, width = resid_ref.shape
    cols = send_ref.shape[1]
    half = width // 2

    @pl.when(step == 0)
    def _():
        hidden = resid_ref[...].astype(jnp.float32) + proj_ref[...].astype(jnp.float32)
        mean_square = jnp.mean(hidden * hidden, axis=1, keepdims=True)
        normed = (hidden * lax.rsqrt(mean_square + 1e-06) * gain_ref[...]).astype(jnp.bfloat16)
        halves_ref[:tokens, :] = normed[:, :half]
        halves_ref[tokens:, :] = normed[:, half:]

    for j in range(half // cols):

        @pl.when(step == j)
        def _():
            send_ref[...] = dot(
                pick_ref[...], halves_ref[:, j * cols : (j + 1) * cols]
            ).astype(jnp.bfloat16)


def route_first(resid, projected, gain, pick, cols=1024):
    tokens, width = resid.shape
    rows, twice = pick.shape
    half = width // 2
    whole = lambda shape: pl.BlockSpec(shape, lambda j: (0,) * len(shape))
    return pl.pallas_call(
        route_first_kernel,
        grid=(half // cols,),
        in_specs=[
            pl.BlockSpec(memory_space=pltpu.VMEM),
            whole((tokens, width)),
            pl.BlockSpec(memory_space=pltpu.VMEM),
            pl.BlockSpec(memory_space=pltpu.VMEM),
        ],
        out_specs=[pl.BlockSpec((rows, cols), lambda j: (0, j)), whole((twice, half))],
        out_shape=[
            pltpu.HBM((rows, half), jnp.bfloat16),
            pltpu.HBM((twice, half), jnp.bfloat16),
        ],
        compiler_params=pltpu.CompilerParams(vmem_limit_bytes=32 * MIB),
        name="route_first",
    )(resid, projected, gain, pick)


def route_second_kernel(halves_ref, pick_ref, ninth_ref, send_ref, extra_ref):
    step = pl.program_id(0)
    twice, half = halves_ref.shape
    cols = send_ref.shape[1]
    experts, tokens = ninth_ref.shape
    steps = half // cols

    for j in range(steps):

        @pl.when(step == j)
        def _():
            part = halves_ref[:, j * cols : (j + 1) * cols]
            send_ref[...] = dot(pick_ref[...], part).astype(jnp.bfloat16)
            for side in range(2):
                piece = dot(ninth_ref[...], part[side * tokens : (side + 1) * tokens])
                for b in range(cols // 128):
                    extra_ref[b, pl.ds(side * steps + j, experts, stride=SLOTS), :] = piece[
                        :, b * 128 : (b + 1) * 128
                    ]

    @pl.when(step == steps)
    def _():
        for b in range(cols // 128):
            send_ref[:, b * 128 : (b + 1) * 128] = extra_ref[b].astype(jnp.bfloat16)


def route_second(halves, pick, ninth):
    twice, half = halves.shape
    rows = pick.shape[0]
    cols = 2 * half // SLOTS
    whole = lambda shape: pl.BlockSpec(shape, lambda j: (0,) * len(shape))
    return pl.pallas_call(
        route_second_kernel,
        grid=(half // cols + 1,),
        in_specs=[
            whole((twice, half)),
            whole(pick.shape),
            whole(ninth.shape),
        ],
        out_specs=pl.BlockSpec((rows, cols), lambda j: (0, j)),
        out_shape=pltpu.HBM((rows, half + cols), jnp.bfloat16),
        scratch_shapes=[pltpu.VMEM((cols // 128, rows, 128), jnp.float32)],
        compiler_params=pltpu.CompilerParams(vmem_limit_bytes=32 * MIB),
        name="route_second",
    )(halves, pick, ninth)


def weights_kernel(halves_ref, router_ref, rank_ref, zero_ref, one_ref, ninth_ref):
    tokens, experts = rank_ref.shape
    half = halves_ref.shape[1]
    rank = rank_ref[...]
    named = rank > 0.0
    logits = dot(halves_ref[:tokens, :], router_ref[:half, :]) + dot(
        halves_ref[tokens:, :], router_ref[half:, :]
    )
    top = jnp.max(jnp.where(named, logits, -jnp.inf), axis=1, keepdims=True)
    raised = jnp.where(named, jnp.exp(jnp.where(named, logits, top) - top), 0.0)
    weight = raised / jnp.sum(raised, axis=1, keepdims=True)
    high = weight.astype(jnp.bfloat16)
    low = (weight - high.astype(jnp.float32)).astype(jnp.bfloat16)
    spread = spread_flags(experts, 1)
    wide_rank = dot(rank.astype(jnp.bfloat16), spread)
    row = lax.broadcasted_iota(jnp.int32, wide_rank.shape, 1) % SLOTS
    slot = (row % HALF).astype(jnp.float32)
    for term, part in enumerate((high, low)):
        place = pl.ds(term * tokens, tokens)
        wide = dot(part, spread)
        for chunk in range(2):
            kept = jnp.where(wide_rank == slot + float(1 + HALF * chunk), wide, 0.0)
            main_ref = (zero_ref, one_ref)[chunk]
            main_ref[0, place, :] = jnp.where(row < HALF, kept, 0.0).astype(jnp.bfloat16)
            main_ref[1, place, :] = jnp.where(row >= HALF, kept, 0.0).astype(jnp.bfloat16)
        ninth_ref[place, :] = jnp.where(
            rank == SLOTS + 1.0, part.astype(jnp.float32), 0.0
        ).astype(jnp.bfloat16)


def weights(halves, router, rank):
    tokens, experts = rank.shape
    return pl.pallas_call(
        weights_kernel,
        out_shape=[
            pltpu.HBM((2, 2 * tokens, experts * SLOTS), jnp.bfloat16),
            pltpu.VMEM((2, 2 * tokens, experts * SLOTS), jnp.bfloat16),
            pltpu.VMEM((2 * tokens, experts), jnp.bfloat16),
        ],
        compiler_params=pltpu.CompilerParams(vmem_limit_bytes=32 * MIB),
        name="weights",
    )(halves, router, rank)


def sort_rows():
    to = lax.broadcasted_iota(jnp.int32, (GROUP, GROUP), 0)
    source = lax.broadcasted_iota(jnp.int32, (GROUP, GROUP), 1)
    count = GROUP // 2
    side, index = to // count, to % count
    return flags(source == index // HALF * SLOTS + side * HALF + index % HALF)


def sort_pieces():
    to = lax.broadcasted_iota(jnp.int32, (GROUP, GROUP), 0)
    source = lax.broadcasted_iota(jnp.int32, (GROUP, GROUP), 1)
    count = GROUP // SLOTS
    return flags(source == to % count * SLOTS + to // count)


def dot_tn(a, b):
    return lax.dot_general(a, b, (((0,), (0,)), ((), ())), preferred_element_type=jnp.float32)


def expert_kernel(*refs, deep, ninth):
    rows_ref, refs = refs[0], refs[1:]
    gate_ref, up_ref, first_ref, second_ref, out_ref = refs[:5]
    token_ref, gate_acc, up_acc, act_ref, piece_ref = refs[5:]
    step = pl.program_id(0)
    groups = out_ref.shape[0] // GROUP
    count = GROUP // 2
    few = GROUP // SLOTS
    main = groups * count
    cols = out_ref.shape[1]
    half = rows_ref.shape[1] - (cols if ninth else 0)
    deep_cols = gate_ref.shape[1]
    steps = half // cols

    @pl.when(step < groups)
    def _():
        g = jnp.minimum(step, groups - 1)
        place = pl.ds(pl.multiple_of(g * count, count), count)
        lined = dot(sort_rows(), rows_ref[:, :half]).astype(jnp.bfloat16)
        for k in range(deep):
            side, lane = divmod(k * deep_cols, half)
            token_ref[k, place, :] = lined[
                side * count : (side + 1) * count, lane : lane + deep_cols
            ]
        if ninth:
            place = pl.ds(pl.multiple_of(main + g * few, few), few)
            pieces = dot(sort_pieces(), rows_ref[:, half:]).astype(jnp.bfloat16)
            for j in range(SLOTS):
                k, lane = divmod(j * cols, deep_cols)
                token_ref[k, place, lane : lane + cols] = pieces[j * few : (j + 1) * few]

    start = groups

    @pl.when(step == start)
    def _():
        gate_acc[...] = dot(token_ref[0], gate_ref[0])
        up_acc[...] = dot(token_ref[0], up_ref[0])

    @pl.when((step > start) & (step < start + deep))
    def _():
        rows = token_ref[jnp.clip(step - start, 0, deep - 1)]
        gate_acc[...] += dot(rows, gate_ref[0])
        up_acc[...] += dot(rows, up_ref[0])

    @pl.when(step == start + deep - 1)
    def _():
        gate_val = gate_acc[...]
        act_ref[...] = (gate_val / (1.0 + jnp.exp(-gate_val)) * up_acc[...]).astype(jnp.bfloat16)

    start = groups + deep

    @pl.when((step >= start) & (step < start + steps))
    def _():
        act = act_ref[...]
        sides = [dot(act, ref[0]).astype(jnp.bfloat16) for ref in (first_ref, second_ref)]
        order = sort_rows()
        for g in range(groups):
            part = jnp.concatenate([side[g * count : (g + 1) * count] for side in sides], axis=0)
            out_ref[g * GROUP : (g + 1) * GROUP, :] = dot_tn(order, part).astype(jnp.bfloat16)
        if ninth:
            j = jnp.clip(step - start, 0, steps - 1)
            for which, side in enumerate(sides):
                piece_ref[j + which * steps] = side[main:]

    if ninth:

        @pl.when(step == start + steps)
        def _():
            order = sort_pieces()
            for g in range(groups):
                part = jnp.concatenate(
                    [piece_ref[j, g * few : (g + 1) * few, :] for j in range(SLOTS)], axis=0
                )
                out_ref[g * GROUP : (g + 1) * GROUP, :] = dot_tn(order, part).astype(jnp.bfloat16)


def expert(rows, w_gate, w_up, w_down, ninth, deep=4):
    tall, columns = rows.shape
    _, width, hidden = w_gate.shape
    half, cols = width // 2, width // SLOTS
    assert columns == half + (cols if ninth else 0) and tall % GROUP == 0
    groups, steps = tall // GROUP, half // cols
    main = tall // 2 + (tall // SLOTS if ninth else 0)
    at = groups + deep
    inner = lambda s, begin, count: jnp.clip(s - begin, 0, count - 1)
    weight = pl.BlockSpec((1, width // deep, hidden), lambda s: (0, inner(s, groups, deep), 0))
    return pl.pallas_call(
        functools.partial(expert_kernel, deep=deep, ninth=ninth),
        grid=(at + steps + ninth,),
        in_specs=[
            pl.BlockSpec((GROUP, columns), lambda s: (inner(s, 0, groups), 0)),
            weight,
            weight,
            pl.BlockSpec((1, hidden, cols), lambda s: (0, 0, inner(s, at, steps))),
            pl.BlockSpec((1, hidden, cols), lambda s: (0, 0, steps + inner(s, at, steps))),
        ],
        out_specs=pl.BlockSpec((tall, cols), lambda s: (0, inner(s, at, steps + ninth))),
        out_shape=pltpu.HBM(rows.shape, jnp.bfloat16),
        scratch_shapes=[
            pltpu.VMEM((deep, main, width // deep), jnp.bfloat16),
            pltpu.VMEM((main, hidden), jnp.float32),
            pltpu.VMEM((main, hidden), jnp.float32),
            pltpu.VMEM((main, hidden), jnp.bfloat16),
            pltpu.VMEM((SLOTS, tall // SLOTS, cols), jnp.bfloat16),
        ],
        compiler_params=pltpu.CompilerParams(vmem_limit_bytes=40 * MIB),
        name="expert_second" if ninth else "expert_first",
    )(rows, w_gate, w_up, w_down, w_down)


def combine_first_kernel(rows_ref, weight_ref, *refs):
    resids, projs, out_ref = refs[:2], refs[2:4], refs[4]
    tokens = out_ref.shape[1]
    for side in range(2):
        both = dot(weight_ref[side], rows_ref[...])
        hidden = resids[side][...].astype(jnp.float32) + projs[side][...].astype(jnp.float32)
        out_ref[side] = hidden + (both[:tokens] + both[tokens:])


def combine_first(rows, main_weight, resid, projected):
    tokens, width = resid.shape
    tall, half = rows.shape
    cols = width // SLOTS
    steps = half // cols
    first = pl.BlockSpec((tokens, cols), lambda j: (0, j))
    second = pl.BlockSpec((tokens, cols), lambda j: (0, steps + j))
    return pl.pallas_call(
        combine_first_kernel,
        grid=(steps,),
        in_specs=[
            pl.BlockSpec((tall, cols), lambda j: (0, j)),
            pl.BlockSpec(main_weight.shape, lambda j: (0, 0, 0)),
            first,
            second,
            first,
            second,
        ],
        out_specs=pl.BlockSpec((2, tokens, cols), lambda j: (0, 0, j)),
        out_shape=pltpu.HBM((2, tokens, half), jnp.float32),
        compiler_params=pltpu.CompilerParams(vmem_limit_bytes=32 * MIB),
        name="combine_first",
    )(rows, main_weight, resid, resid, projected, projected)


def combine_second_kernel(
    rows_hbm, partial_hbm, weight_ref, ninth_ref, out_hbm,
    rows_ref, partial_ref, out_ref, piece_ref, row_sems, partial_sems, out_sems,
):
    tall, columns = rows_hbm.shape
    tokens, width = out_hbm.shape
    half = width // 2
    small = columns - half
    steps = half // small
    groups, few = tall // GROUP, GROUP // SLOTS

    def rows_copy(j):
        lanes = pl.ds(j * small, small)
        return pltpu.make_async_copy(rows_hbm.at[:, lanes], rows_ref.at[j], row_sems.at[j])

    def partial_copy(j):
        lanes = pl.ds(j * small, small)
        return pltpu.make_async_copy(
            partial_hbm.at[:, :, lanes], partial_ref.at[j], partial_sems.at[j]
        )

    def out_copy(piece):
        lanes = pl.ds(piece * small, small)
        return pltpu.make_async_copy(out_ref.at[piece], out_hbm.at[:, lanes], out_sems.at[piece])

    rows_copy(steps).start()
    for j in range(steps):
        rows_copy(j).start()
        partial_copy(j).start()
    rows_copy(steps).wait()
    order = sort_pieces()
    for g in range(groups):
        pieces = dot(order, rows_ref[steps, g * GROUP : (g + 1) * GROUP, :]).astype(jnp.bfloat16)
        for j in range(SLOTS):
            piece_ref[j, g * few : (g + 1) * few, :] = pieces[j * few : (j + 1) * few]
    for j in range(steps):
        rows_copy(j).wait()
        partial_copy(j).wait()
        for side in range(2):
            piece = side * steps + j
            both = dot(weight_ref[side], rows_ref[j]) + dot(ninth_ref[...], piece_ref[piece])
            out_ref[piece] = (partial_ref[j, side] + (both[:tokens] + both[tokens:])).astype(
                jnp.bfloat16
            )
            out_copy(piece).start()
    for piece in range(2 * steps):
        out_copy(piece).wait()


def combine_second(rows, main_weight, ninth_weight, partial):
    _, tokens, half = partial.shape
    tall, columns = rows.shape
    small = columns - half
    steps = half // small
    return pl.pallas_call(
        combine_second_kernel,
        in_specs=[
            pl.BlockSpec(memory_space=pltpu.HBM),
            pl.BlockSpec(memory_space=pltpu.HBM),
            pl.BlockSpec(memory_space=pltpu.VMEM),
            pl.BlockSpec(memory_space=pltpu.VMEM),
        ],
        out_specs=pl.BlockSpec(memory_space=pltpu.HBM),
        out_shape=jax.ShapeDtypeStruct((tokens, 2 * half), jnp.bfloat16),
        scratch_shapes=[
            pltpu.VMEM((steps + 1, tall, small), jnp.bfloat16),
            pltpu.VMEM((steps, 2, tokens, small), jnp.float32),
            pltpu.VMEM((2 * steps, tokens, small), jnp.bfloat16),
            pltpu.VMEM((SLOTS, tall // SLOTS, small), jnp.bfloat16),
            pltpu.SemaphoreType.DMA((steps + 1,)),
            pltpu.SemaphoreType.DMA((steps,)),
            pltpu.SemaphoreType.DMA((2 * steps,)),
        ],
        compiler_params=pltpu.CompilerParams(vmem_limit_bytes=32 * MIB),
        name="combine_second",
    )(rows, partial, main_weight, ninth_weight)


def per_device(
    resid,
    queries,
    span_rotated_keys,
    span_value_rows,
    key_cache,
    prefix_value_cache,
    prefix_len,
    out_weight,
    norm_gain,
    router_weight,
    expert_ids,
    w_gate,
    w_up,
    w_down,
):
    seq_count = lax.axis_size("seq")
    width = resid.shape[2]
    experts = router_weight.shape[1]
    packed = pack(
        queries, span_rotated_keys, span_value_rows, key_cache, prefix_value_cache, seq_count
    )
    packed = lax.all_to_all(packed, "seq", split_axis=0, concat_axis=0, tiled=True)
    projected = lax.psum_scatter(
        attend(prefix_len, packed, in_hbm(out_weight)), "seq", scatter_dimension=0, tiled=True
    )
    projected = in_hbm(projected)
    rank, pick_first, pick_second, ninth = plan(expert_ids[0], experts)
    rank, pick_second, ninth = in_hbm(rank), in_hbm(pick_second), in_hbm(ninth)
    send_first, halves = route_first(resid[0], projected, norm_gain.reshape(1, width), pick_first)

    def exchange(rows):
        blocks = rows.reshape(experts, SLOTS, rows.shape[1])
        return in_hbm(
            lax.all_to_all(
                blocks, ("seq", "exp"), split_axis=0, concat_axis=0, tiled=True
            ).reshape(rows.shape)
        )

    halves = in_hbm(halves)
    w_gate, w_up, w_down = in_hbm(w_gate), in_hbm(w_up), in_hbm(w_down)
    got_first = exchange(send_first)
    got_second = exchange(route_second(halves, pick_second, ninth))
    first_weight, second_weight, ninth_weight = weights(halves, router_weight, rank)
    back_first = exchange(expert(got_first, w_gate, w_up, w_down, False))
    back_second = exchange(expert(got_second, w_gate, w_up, w_down, True))
    partial = combine_first(back_first, in_hbm(first_weight), resid[0], projected)
    return combine_second(back_second, second_weight, ninth_weight, in_hbm(partial))[None]


def solution(mesh):
    in_specs = (
        P("exp", "seq", None),
        P("exp", "seq", None),
        P("exp", "seq", None),
        P("exp", "seq", None),
        P("exp", None, "seq", None),
        P("exp", None, "seq", None),
        P("exp"),
        P("seq", None),
        P(),
        P(),
        P("exp", "seq", None),
        P(("seq", "exp"), None, None),
        P(("seq", "exp"), None, None),
        P(("seq", "exp"), None, None),
    )
    out_specs = P("exp", "seq", None)
    return jax.shard_map(
        per_device, mesh=mesh, in_specs=in_specs, out_specs=out_specs, check_vma=False
    )
```

```python
import functools

import jax
import jax.numpy as jnp
import numpy as np
from jax import lax
from jax.experimental import pallas as pl
from jax.experimental.pallas import tpu as pltpu
from jax.sharding import PartitionSpec as P

QUERY_HEAD_HALF = 32
KEY_VALUE_HEADS = 4
HEAD_SIZE = 128
TOP = 8
SLOTS = 8
HALF = SLOTS // 2
GROUP = 256
MIB = 1 << 20


def dot(a, b):
    return jnp.dot(a, b, preferred_element_type=jnp.float32)


def in_hbm(x):
    return pltpu.with_memory_space_constraint(x, pltpu.HBM)


def dot_nt(a, b):
    return lax.dot_general(a, b, (((1,), (1,)), ((), ())), preferred_element_type=jnp.float32)


def pack_kernel(query_ref, key_ref, value_ref, key_cache_ref, value_cache_ref, out_ref, sems):
    parts = out_ref.shape[0]
    cached, tokens = key_cache_ref.shape[2], query_ref.shape[1]
    lanes = query_ref.shape[2] // parts
    ends = [lanes + i * HEAD_SIZE for i in range(4)]
    copies = []
    for s in range(parts):
        head = s * KEY_VALUE_HEADS // parts
        heads = pl.ds(head * HEAD_SIZE, HEAD_SIZE)
        moves = [
            (query_ref.at[0, :, pl.ds(s * lanes, lanes)], out_ref.at[s, :, pl.ds(0, lanes)]),
            (key_ref.at[0, :, heads], out_ref.at[s, :, pl.ds(ends[0], HEAD_SIZE)]),
            (value_ref.at[0, :, heads], out_ref.at[s, :, pl.ds(ends[1], HEAD_SIZE)]),
            (
                key_cache_ref.at[0, head],
                out_ref.at[s, pl.ds(0, cached), pl.ds(ends[2], HEAD_SIZE)],
            ),
            (
                value_cache_ref.at[0, head],
                out_ref.at[s, pl.ds(cached, tokens - cached), pl.ds(ends[2], HEAD_SIZE)],
            ),
        ]
        for i, (source, target) in enumerate(moves):
            copies.append(pltpu.make_async_copy(source, target, sems.at[s, i]))
    for copy in copies:
        copy.start()
    for copy in copies:
        copy.wait()


def pack(queries, keys, values, key_cache, value_cache, seq_count):
    tokens, width = queries.shape[1:]
    cached = key_cache.shape[2]
    assert 2 * cached == tokens
    lanes = width // seq_count
    return pl.pallas_call(
        pack_kernel,
        in_specs=[pl.BlockSpec(memory_space=pltpu.VMEM)] * 5,
        out_specs=pl.BlockSpec(memory_space=pltpu.HBM),
        out_shape=pltpu.HBM((seq_count, tokens, lanes + 3 * HEAD_SIZE), jnp.bfloat16),
        scratch_shapes=[pltpu.SemaphoreType.DMA((seq_count, 5))],
        name="pack",
    )(queries, keys, values, key_cache, value_cache)


def attend_kernel(
    length_ref, packed_ref, out_weight_hbm, out_hbm,
    key_ref, value_ref, att_ref, out_weight_ref, out_ref, sem, out_sems,
):
    parts, tokens, _ = packed_ref.shape
    lanes, width = out_weight_ref.shape
    heads = lanes // HEAD_SIZE
    cached = tokens // 2
    prefix = parts * cached
    blocks, rows, _ = att_ref.shape
    per_block = rows // tokens
    cols = width // heads
    rate = HEAD_SIZE ** (-0.5) * float(np.log2(np.e))
    fetch = pltpu.make_async_copy(out_weight_hbm, out_weight_ref, sem)
    fetch.start()
    for t in range(parts):
        old = pl.ds(t * cached, cached)
        new = pl.ds(prefix + t * tokens, tokens)
        key_ref[old, :] = packed_ref[t, :cached, lanes + 2 * HEAD_SIZE :]
        value_ref[old, :] = packed_ref[t, cached:, lanes + 2 * HEAD_SIZE :]
        key_ref[new, :] = packed_ref[t, :, lanes : lanes + HEAD_SIZE]
        value_ref[new, :] = packed_ref[t, :, lanes + HEAD_SIZE : lanes + 2 * HEAD_SIZE]

    in_prefix = lax.broadcasted_iota(jnp.int32, (rows, prefix), 1) < length_ref[0]
    causal = lax.broadcasted_iota(jnp.int32, (rows, rows), 1) <= lax.broadcasted_iota(
        jnp.int32, (rows, rows), 0
    )

    def spans_of(i):
        middle = [(prefix, i * rows)] if i else []
        return [(0, prefix)] + middle + [(prefix + i * rows, rows)]

    def score(i, h):
        query = jnp.concatenate(
            [
                packed_ref[i * per_block + t, :, h * HEAD_SIZE : (h + 1) * HEAD_SIZE]
                for t in range(per_block)
            ],
            axis=0,
        )
        return [dot_nt(query, key_ref[pl.ds(start, size), :]) for start, size in spans_of(i)]

    def finish(i, h, scores):
        scores[0] = jnp.where(in_prefix, scores[0], -1e30)
        scores[-1] = jnp.where(causal, scores[-1], -1e30)
        top = functools.reduce(jnp.maximum, [jnp.max(s, axis=1, keepdims=True) for s in scores])
        total, result = 0.0, 0.0
        for s, (start, size) in zip(scores, spans_of(i), strict=True):
            raised = jnp.exp2((s - top) * rate)
            total = total + jnp.sum(raised, axis=1, keepdims=True)
            result = result + dot(raised.astype(jnp.bfloat16), value_ref[pl.ds(start, size), :])
        att_ref[i, :, h * HEAD_SIZE : (h + 1) * HEAD_SIZE] = (result / total).astype(jnp.bfloat16)

    def out_copy(i, j):
        return pltpu.make_async_copy(
            out_ref.at[i, j],
            out_hbm.at[pl.ds(i * rows, rows), pl.ds(j * cols, cols)],
            out_sems.at[i, j],
        )

    def project(i, j):
        out_ref[i, j] = dot(att_ref[i], out_weight_ref[:, j * cols : (j + 1) * cols]).astype(
            jnp.bfloat16
        )
        out_copy(i, j).start()

    units = [(i, h) for i in range(blocks) for h in range(heads)]
    scores = score(*units[0])
    for u, (i, h) in enumerate(units):
        following = score(*units[u + 1]) if u + 1 < len(units) else None
        if i:
            project(i - 1, h)
        finish(i, h, scores)
        scores = following
        if (i, h) == (0, heads - 1):
            fetch.wait()
    for h in range(heads):
        project(blocks - 1, h)
    for i in range(blocks):
        for j in range(heads):
            out_copy(i, j).wait()


def attend(length, packed, out_weight, rows=256):
    parts, tokens, _ = packed.shape
    lanes, width = out_weight.shape
    span = parts * tokens
    total = span + parts * tokens // 2
    heads = lanes // HEAD_SIZE
    return pl.pallas_call(
        attend_kernel,
        in_specs=[
            pl.BlockSpec(memory_space=pltpu.SMEM),
            pl.BlockSpec(memory_space=pltpu.VMEM),
            pl.BlockSpec(memory_space=pltpu.HBM),
        ],
        out_specs=pl.BlockSpec(memory_space=pltpu.HBM),
        out_shape=jax.ShapeDtypeStruct((span, width), jnp.bfloat16),
        scratch_shapes=[
            pltpu.VMEM((total, HEAD_SIZE), jnp.bfloat16),
            pltpu.VMEM((total, HEAD_SIZE), jnp.bfloat16),
            pltpu.VMEM((span // rows, rows, lanes), jnp.bfloat16),
            pltpu.VMEM((lanes, width), jnp.bfloat16),
            pltpu.VMEM((span // rows, heads, rows, width // heads), jnp.bfloat16),
            pltpu.SemaphoreType.DMA,
            pltpu.SemaphoreType.DMA((span // rows, heads)),
        ],
        compiler_params=pltpu.CompilerParams(vmem_limit_bytes=48 * MIB),
        name="attend",
    )(length, packed, out_weight)


def named_mask(ids_ref, experts):
    tokens = ids_ref.shape[0]
    lane = lax.broadcasted_iota(jnp.int32, (tokens, experts), 1)
    named = ids_ref[:, 0:1] == lane
    for k in range(1, TOP):
        named = named | (ids_ref[:, k : k + 1] == lane)
    return named


def flags(condition):
    return jnp.where(condition, 1.0, 0.0).astype(jnp.bfloat16)


def spread_flags(experts, axis):
    shape = (experts * SLOTS, experts) if axis == 0 else (experts, experts * SLOTS)
    owner = lax.broadcasted_iota(jnp.int32, shape, axis) // SLOTS
    return flags(owner == lax.broadcasted_iota(jnp.int32, shape, 1 - axis))


def plan_kernel(ids_ref, rank_ref, zero_ref, one_ref, ninth_ref):
    tokens, experts = rank_ref.shape
    named = named_mask(ids_ref, experts)
    earlier = flags(
        lax.broadcasted_iota(jnp.int32, (tokens, tokens), 0)
        > lax.broadcasted_iota(jnp.int32, (tokens, tokens), 1)
    )
    rank = jnp.where(named, dot(earlier, flags(named)) + 1.0, 0.0)
    rank_ref[...] = rank
    narrow = rank.astype(jnp.bfloat16)
    wide = dot_nt(spread_flags(experts, 0), narrow)
    row = lax.broadcasted_iota(jnp.int32, wide.shape, 0) % SLOTS
    slot = (row % HALF).astype(jnp.float32)
    for chunk in range(2):
        hit = wide == slot + float(1 + HALF * chunk)
        pick_ref = (zero_ref, one_ref)[chunk]
        pick_ref[:, :tokens] = flags(hit & (row < HALF))
        pick_ref[:, tokens:] = flags(hit & (row >= HALF))
    same = flags(
        lax.broadcasted_iota(jnp.int32, (experts, experts), 0)
        == lax.broadcasted_iota(jnp.int32, (experts, experts), 1)
    )
    ninth_ref[...] = flags(dot_nt(same, narrow) == SLOTS + 1.0)


def plan(ids, experts):
    tokens = ids.shape[0]
    return pl.pallas_call(
        plan_kernel,
        out_shape=[
            pltpu.HBM((tokens, experts), jnp.float32),
            pltpu.VMEM((experts * SLOTS, 2 * tokens), jnp.bfloat16),
            pltpu.HBM((experts * SLOTS, 2 * tokens), jnp.bfloat16),
            pltpu.HBM((experts, tokens), jnp.bfloat16),
        ],
        name="plan",
    )(ids)


def route_first_kernel(resid_ref, proj_ref, gain_ref, pick_ref, send_ref, halves_ref):
    step = pl.program_id(0)
    tokens, width = resid_ref.shape
    cols = send_ref.shape[1]
    half = width // 2

    @pl.when(step == 0)
    def _():
        hidden = resid_ref[...].astype(jnp.float32) + proj_ref[...].astype(jnp.float32)
        mean_square = jnp.mean(hidden * hidden, axis=1, keepdims=True)
        normed = (hidden * lax.rsqrt(mean_square + 1e-06) * gain_ref[...]).astype(jnp.bfloat16)
        halves_ref[:tokens, :] = normed[:, :half]
        halves_ref[tokens:, :] = normed[:, half:]

    for j in range(half // cols):

        @pl.when(step == j)
        def _():
            send_ref[...] = dot(
                pick_ref[...], halves_ref[:, j * cols : (j + 1) * cols]
            ).astype(jnp.bfloat16)


def route_first(resid, projected, gain, pick, cols=1024):
    tokens, width = resid.shape
    rows, twice = pick.shape
    half = width // 2
    whole = lambda shape: pl.BlockSpec(shape, lambda j: (0,) * len(shape))
    return pl.pallas_call(
        route_first_kernel,
        grid=(half // cols,),
        in_specs=[
            pl.BlockSpec(memory_space=pltpu.VMEM),
            whole((tokens, width)),
            pl.BlockSpec(memory_space=pltpu.VMEM),
            pl.BlockSpec(memory_space=pltpu.VMEM),
        ],
        out_specs=[pl.BlockSpec((rows, cols), lambda j: (0, j)), whole((twice, half))],
        out_shape=[
            pltpu.HBM((rows, half), jnp.bfloat16),
            pltpu.HBM((twice, half), jnp.bfloat16),
        ],
        compiler_params=pltpu.CompilerParams(vmem_limit_bytes=32 * MIB),
        name="route_first",
    )(resid, projected, gain, pick)


def route_second_kernel(halves_ref, pick_ref, ninth_ref, send_ref, extra_ref):
    step = pl.program_id(0)
    twice, half = halves_ref.shape
    cols = send_ref.shape[1]
    experts, tokens = ninth_ref.shape
    steps = half // cols

    for j in range(steps):

        @pl.when(step == j)
        def _():
            part = halves_ref[:, j * cols : (j + 1) * cols]
            send_ref[...] = dot(pick_ref[...], part).astype(jnp.bfloat16)
            for side in range(2):
                piece = dot(ninth_ref[...], part[side * tokens : (side + 1) * tokens])
                for b in range(cols // 128):
                    extra_ref[b, pl.ds(side * steps + j, experts, stride=SLOTS), :] = piece[
                        :, b * 128 : (b + 1) * 128
                    ]

    @pl.when(step == steps)
    def _():
        for b in range(cols // 128):
            send_ref[:, b * 128 : (b + 1) * 128] = extra_ref[b].astype(jnp.bfloat16)


def route_second(halves, pick, ninth):
    twice, half = halves.shape
    rows = pick.shape[0]
    cols = 2 * half // SLOTS
    whole = lambda shape: pl.BlockSpec(shape, lambda j: (0,) * len(shape))
    return pl.pallas_call(
        route_second_kernel,
        grid=(half // cols + 1,),
        in_specs=[
            whole((twice, half)),
            whole(pick.shape),
            whole(ninth.shape),
        ],
        out_specs=pl.BlockSpec((rows, cols), lambda j: (0, j)),
        out_shape=pltpu.HBM((rows, half + cols), jnp.bfloat16),
        scratch_shapes=[pltpu.VMEM((cols // 128, rows, 128), jnp.float32)],
        compiler_params=pltpu.CompilerParams(vmem_limit_bytes=32 * MIB),
        name="route_second",
    )(halves, pick, ninth)


def weights_kernel(halves_ref, router_ref, rank_ref, zero_ref, one_ref, ninth_ref):
    tokens, experts = rank_ref.shape
    half = halves_ref.shape[1]
    rank = rank_ref[...]
    named = rank > 0.0
    logits = dot(halves_ref[:tokens, :], router_ref[:half, :]) + dot(
        halves_ref[tokens:, :], router_ref[half:, :]
    )
    top = jnp.max(jnp.where(named, logits, -jnp.inf), axis=1, keepdims=True)
    raised = jnp.where(named, jnp.exp(jnp.where(named, logits, top) - top), 0.0)
    weight = raised / jnp.sum(raised, axis=1, keepdims=True)
    high = weight.astype(jnp.bfloat16)
    low = (weight - high.astype(jnp.float32)).astype(jnp.bfloat16)
    spread = spread_flags(experts, 1)
    wide_rank = dot(rank.astype(jnp.bfloat16), spread)
    row = lax.broadcasted_iota(jnp.int32, wide_rank.shape, 1) % SLOTS
    slot = (row % HALF).astype(jnp.float32)
    for term, part in enumerate((high, low)):
        place = pl.ds(term * tokens, tokens)
        wide = dot(part, spread)
        for chunk in range(2):
            kept = jnp.where(wide_rank == slot + float(1 + HALF * chunk), wide, 0.0)
            main_ref = (zero_ref, one_ref)[chunk]
            main_ref[0, place, :] = jnp.where(row < HALF, kept, 0.0).astype(jnp.bfloat16)
            main_ref[1, place, :] = jnp.where(row >= HALF, kept, 0.0).astype(jnp.bfloat16)
        ninth_ref[place, :] = jnp.where(
            rank == SLOTS + 1.0, part.astype(jnp.float32), 0.0
        ).astype(jnp.bfloat16)


def weights(halves, router, rank):
    tokens, experts = rank.shape
    return pl.pallas_call(
        weights_kernel,
        out_shape=[
            pltpu.HBM((2, 2 * tokens, experts * SLOTS), jnp.bfloat16),
            pltpu.VMEM((2, 2 * tokens, experts * SLOTS), jnp.bfloat16),
            pltpu.VMEM((2 * tokens, experts), jnp.bfloat16),
        ],
        compiler_params=pltpu.CompilerParams(vmem_limit_bytes=32 * MIB),
        name="weights",
    )(halves, router, rank)


def sort_rows():
    to = lax.broadcasted_iota(jnp.int32, (GROUP, GROUP), 0)
    source = lax.broadcasted_iota(jnp.int32, (GROUP, GROUP), 1)
    count = GROUP // 2
    side, index = to // count, to % count
    return flags(source == index // HALF * SLOTS + side * HALF + index % HALF)


def sort_pieces():
    to = lax.broadcasted_iota(jnp.int32, (GROUP, GROUP), 0)
    source = lax.broadcasted_iota(jnp.int32, (GROUP, GROUP), 1)
    count = GROUP // SLOTS
    return flags(source == to % count * SLOTS + to // count)


def dot_tn(a, b):
    return lax.dot_general(a, b, (((0,), (0,)), ((), ())), preferred_element_type=jnp.float32)


def expert_kernel(*refs, deep, ninth):
    rows_ref, refs = refs[0], refs[1:]
    gate_ref, up_ref, first_ref, second_ref, out_ref = refs[:5]
    token_ref, gate_acc, up_acc, act_ref, piece_ref = refs[5:]
    step = pl.program_id(0)
    groups = out_ref.shape[0] // GROUP
    count = GROUP // 2
    few = GROUP // SLOTS
    main = groups * count
    cols = out_ref.shape[1]
    half = rows_ref.shape[1] - (cols if ninth else 0)
    deep_cols = gate_ref.shape[1]
    steps = half // cols

    @pl.when(step < groups)
    def _():
        g = jnp.minimum(step, groups - 1)
        place = pl.ds(pl.multiple_of(g * count, count), count)
        lined = dot(sort_rows(), rows_ref[:, :half]).astype(jnp.bfloat16)
        for k in range(deep):
            side, lane = divmod(k * deep_cols, half)
            token_ref[k, place, :] = lined[
                side * count : (side + 1) * count, lane : lane + deep_cols
            ]
        if ninth:
            place = pl.ds(pl.multiple_of(main + g * few, few), few)
            pieces = dot(sort_pieces(), rows_ref[:, half:]).astype(jnp.bfloat16)
            for j in range(SLOTS):
                k, lane = divmod(j * cols, deep_cols)
                token_ref[k, place, lane : lane + cols] = pieces[j * few : (j + 1) * few]

    start = groups

    @pl.when(step == start)
    def _():
        gate_acc[...] = dot(token_ref[0], gate_ref[0])
        up_acc[...] = dot(token_ref[0], up_ref[0])

    @pl.when((step > start) & (step < start + deep))
    def _():
        rows = token_ref[jnp.clip(step - start, 0, deep - 1)]
        gate_acc[...] += dot(rows, gate_ref[0])
        up_acc[...] += dot(rows, up_ref[0])

    @pl.when(step == start + deep - 1)
    def _():
        gate_val = gate_acc[...]
        act_ref[...] = (gate_val / (1.0 + jnp.exp(-gate_val)) * up_acc[...]).astype(jnp.bfloat16)

    start = groups + deep

    @pl.when((step >= start) & (step < start + steps))
    def _():
        act = act_ref[...]
        sides = [dot(act, ref[0]).astype(jnp.bfloat16) for ref in (first_ref, second_ref)]
        order = sort_rows()
        for g in range(groups):
            part = jnp.concatenate([side[g * count : (g + 1) * count] for side in sides], axis=0)
            out_ref[g * GROUP : (g + 1) * GROUP, :] = dot_tn(order, part).astype(jnp.bfloat16)
        if ninth:
            j = jnp.clip(step - start, 0, steps - 1)
            for which, side in enumerate(sides):
                piece_ref[j + which * steps] = side[main:]

    if ninth:

        @pl.when(step == start + steps)
        def _():
            order = sort_pieces()
            for g in range(groups):
                part = jnp.concatenate(
                    [piece_ref[j, g * few : (g + 1) * few, :] for j in range(SLOTS)], axis=0
                )
                out_ref[g * GROUP : (g + 1) * GROUP, :] = dot_tn(order, part).astype(jnp.bfloat16)


def expert(rows, w_gate, w_up, w_down, ninth, deep=4):
    tall, columns = rows.shape
    _, width, hidden = w_gate.shape
    half, cols = width // 2, width // SLOTS
    assert columns == half + (cols if ninth else 0) and tall % GROUP == 0
    groups, steps = tall // GROUP, half // cols
    main = tall // 2 + (tall // SLOTS if ninth else 0)
    at = groups + deep
    inner = lambda s, begin, count: jnp.clip(s - begin, 0, count - 1)
    weight = pl.BlockSpec((1, width // deep, hidden), lambda s: (0, inner(s, groups, deep), 0))
    return pl.pallas_call(
        functools.partial(expert_kernel, deep=deep, ninth=ninth),
        grid=(at + steps + ninth,),
        in_specs=[
            pl.BlockSpec((GROUP, columns), lambda s: (inner(s, 0, groups), 0)),
            weight,
            weight,
            pl.BlockSpec((1, hidden, cols), lambda s: (0, 0, inner(s, at, steps))),
            pl.BlockSpec((1, hidden, cols), lambda s: (0, 0, steps + inner(s, at, steps))),
        ],
        out_specs=pl.BlockSpec((tall, cols), lambda s: (0, inner(s, at, steps + ninth))),
        out_shape=pltpu.HBM(rows.shape, jnp.bfloat16),
        scratch_shapes=[
            pltpu.VMEM((deep, main, width // deep), jnp.bfloat16),
            pltpu.VMEM((main, hidden), jnp.float32),
            pltpu.VMEM((main, hidden), jnp.float32),
            pltpu.VMEM((main, hidden), jnp.bfloat16),
            pltpu.VMEM((SLOTS, tall // SLOTS, cols), jnp.bfloat16),
        ],
        compiler_params=pltpu.CompilerParams(vmem_limit_bytes=40 * MIB),
        name="expert_second" if ninth else "expert_first",
    )(rows, w_gate, w_up, w_down, w_down)


def combine_first_kernel(rows_ref, weight_ref, *refs):
    resids, projs, out_ref = refs[:2], refs[2:4], refs[4]
    tokens = out_ref.shape[1]
    for side in range(2):
        both = dot(weight_ref[side], rows_ref[...])
        hidden = resids[side][...].astype(jnp.float32) + projs[side][...].astype(jnp.float32)
        out_ref[side] = hidden + (both[:tokens] + both[tokens:])


def combine_first(rows, main_weight, resid, projected):
    tokens, width = resid.shape
    tall, half = rows.shape
    cols = width // SLOTS
    steps = half // cols
    first = pl.BlockSpec((tokens, cols), lambda j: (0, j))
    second = pl.BlockSpec((tokens, cols), lambda j: (0, steps + j))
    return pl.pallas_call(
        combine_first_kernel,
        grid=(steps,),
        in_specs=[
            pl.BlockSpec((tall, cols), lambda j: (0, j)),
            pl.BlockSpec(main_weight.shape, lambda j: (0, 0, 0)),
            first,
            second,
            first,
            second,
        ],
        out_specs=pl.BlockSpec((2, tokens, cols), lambda j: (0, 0, j)),
        out_shape=pltpu.HBM((2, tokens, half), jnp.float32),
        compiler_params=pltpu.CompilerParams(vmem_limit_bytes=32 * MIB),
        name="combine_first",
    )(rows, main_weight, resid, resid, projected, projected)


def combine_second_kernel(
    rows_hbm, partial_hbm, weight_ref, ninth_ref, out_hbm,
    rows_ref, partial_ref, out_ref, piece_ref, row_sems, partial_sems, out_sems,
):
    tall, columns = rows_hbm.shape
    tokens, width = out_hbm.shape
    half = width // 2
    small = columns - half
    steps = half // small
    groups, few = tall // GROUP, GROUP // SLOTS

    def rows_copy(j):
        lanes = pl.ds(j * small, small)
        return pltpu.make_async_copy(rows_hbm.at[:, lanes], rows_ref.at[j], row_sems.at[j])

    def partial_copy(j):
        lanes = pl.ds(j * small, small)
        return pltpu.make_async_copy(
            partial_hbm.at[:, :, lanes], partial_ref.at[j], partial_sems.at[j]
        )

    def out_copy(piece):
        lanes = pl.ds(piece * small, small)
        return pltpu.make_async_copy(out_ref.at[piece], out_hbm.at[:, lanes], out_sems.at[piece])

    rows_copy(steps).start()
    for j in range(steps):
        rows_copy(j).start()
        partial_copy(j).start()
    rows_copy(steps).wait()
    order = sort_pieces()
    for g in range(groups):
        pieces = dot(order, rows_ref[steps, g * GROUP : (g + 1) * GROUP, :]).astype(jnp.bfloat16)
        for j in range(SLOTS):
            piece_ref[j, g * few : (g + 1) * few, :] = pieces[j * few : (j + 1) * few]
    for j in range(steps):
        rows_copy(j).wait()
        partial_copy(j).wait()
        for side in range(2):
            piece = side * steps + j
            both = dot(weight_ref[side], rows_ref[j]) + dot(ninth_ref[...], piece_ref[piece])
            out_ref[piece] = (partial_ref[j, side] + (both[:tokens] + both[tokens:])).astype(
                jnp.bfloat16
            )
            out_copy(piece).start()
    for piece in range(2 * steps):
        out_copy(piece).wait()


def combine_second(rows, main_weight, ninth_weight, partial):
    _, tokens, half = partial.shape
    tall, columns = rows.shape
    small = columns - half
    steps = half // small
    return pl.pallas_call(
        combine_second_kernel,
        in_specs=[
            pl.BlockSpec(memory_space=pltpu.HBM),
            pl.BlockSpec(memory_space=pltpu.HBM),
            pl.BlockSpec(memory_space=pltpu.VMEM),
            pl.BlockSpec(memory_space=pltpu.VMEM),
        ],
        out_specs=pl.BlockSpec(memory_space=pltpu.HBM),
        out_shape=jax.ShapeDtypeStruct((tokens, 2 * half), jnp.bfloat16),
        scratch_shapes=[
            pltpu.VMEM((steps + 1, tall, small), jnp.bfloat16),
            pltpu.VMEM((steps, 2, tokens, small), jnp.float32),
            pltpu.VMEM((2 * steps, tokens, small), jnp.bfloat16),
            pltpu.VMEM((SLOTS, tall // SLOTS, small), jnp.bfloat16),
            pltpu.SemaphoreType.DMA((steps + 1,)),
            pltpu.SemaphoreType.DMA((steps,)),
            pltpu.SemaphoreType.DMA((2 * steps,)),
        ],
        compiler_params=pltpu.CompilerParams(vmem_limit_bytes=32 * MIB),
        name="combine_second",
    )(rows, partial, main_weight, ninth_weight)


def per_device(
    resid,
    queries,
    span_rotated_keys,
    span_value_rows,
    key_cache,
    prefix_value_cache,
    prefix_len,
    out_weight,
    norm_gain,
    router_weight,
    expert_ids,
    w_gate,
    w_up,
    w_down,
):
    seq_count = lax.axis_size("seq")
    width = resid.shape[2]
    experts = router_weight.shape[1]
    packed = pack(
        queries, span_rotated_keys, span_value_rows, key_cache, prefix_value_cache, seq_count
    )
    packed = lax.all_to_all(packed, "seq", split_axis=0, concat_axis=0, tiled=True)
    projected = lax.psum_scatter(
        attend(prefix_len, packed, in_hbm(out_weight)), "seq", scatter_dimension=0, tiled=True
    )
    projected = in_hbm(projected)
    rank, pick_first, pick_second, ninth = plan(expert_ids[0], experts)
    rank, pick_second, ninth = in_hbm(rank), in_hbm(pick_second), in_hbm(ninth)
    send_first, halves = route_first(resid[0], projected, norm_gain.reshape(1, width), pick_first)

    def exchange(rows):
        blocks = rows.reshape(experts, SLOTS, rows.shape[1])
        return in_hbm(
            lax.all_to_all(
                blocks, ("seq", "exp"), split_axis=0, concat_axis=0, tiled=True
            ).reshape(rows.shape)
        )

    halves = in_hbm(halves)
    w_gate, w_up, w_down = in_hbm(w_gate), in_hbm(w_up), in_hbm(w_down)
    got_first = exchange(send_first)
    got_second = exchange(route_second(halves, pick_second, ninth))
    first_weight, second_weight, ninth_weight = weights(halves, router_weight, rank)
    back_first = exchange(expert(got_first, w_gate, w_up, w_down, False))
    back_second = exchange(expert(got_second, w_gate, w_up, w_down, True))
    partial = combine_first(back_first, in_hbm(first_weight), resid[0], projected)
    return combine_second(back_second, second_weight, ninth_weight, in_hbm(partial))[None]


def solution(mesh):
    in_specs = (
        P("exp", "seq", None),
        P("exp", "seq", None),
        P("exp", "seq", None),
        P("exp", "seq", None),
        P("exp", None, "seq", None),
        P("exp", None, "seq", None),
        P("exp"),
        P("seq", None),
        P(),
        P(),
        P("exp", "seq", None),
        P(("seq", "exp"), None, None),
        P(("seq", "exp"), None, None),
        P(("seq", "exp"), None, None),
    )
    out_specs = P("exp", "seq", None)
    return jax.shard_map(
        per_device, mesh=mesh, in_specs=in_specs, out_specs=out_specs, check_vma=False
    )
```
